256 devices in a mesh: grp: 8 (over x, y_lo), wide: 32 (over y_hi, z, core).
Axes of the slice: x: 4, y: 4 (y_hi: 2, y_lo: 2; y = y_hi * 2 + y_lo), z: 8, core: 2. Of those that a mesh axis runs over, the one named last changes fastest.
Arguments:
- src_rows: float32 [262144, 400], P(('grp', 'wide')), may hold values from -16 to 16
- src_accum: float32 [262144], P(('grp', 'wide')), may hold values from 0.1 to 4
- dst_rows: float32 [16384, 400], P(('grp', 'wide')), may hold values from -1.5 to 1.5
- dst_accum: float32 [16384], P(('grp', 'wide')), may hold values from 0.1 to 4
- relations: float32 [1024, 400], replicated, may hold values from -4 to 4
- rel_ids: int32 [2, 262144], P(None, ('grp', 'wide')), may hold values from 0 to 1023
- targets: int32 [2, 262144], P(None, ('grp', 'wide')), may hold values from 0 to 2047
Outputs:
- new_src: float32 [262144, 400], P(('grp', 'wide'))
- new_src_accum: float32 [262144], P(('grp', 'wide'))
- new_dst: float32 [16384, 400], P(('grp', 'wide'))
- new_dst_accum: float32 [16384], P(('grp', 'wide'))
- edge_loss: float32 [2, 262144], P(None, ('grp', 'wide'))
The draws below stay inside these ranges and needn't reach their ends.
All inputs are finite; a program needn't handle non-finite values.
Results may differ from the reference program's by a relative error of at most 0.009.
Values may be sent and summed in bfloat16 or wider, within the bound.
A program may use at most 64 MiB of HBM per device.

```python
import math
import jax
import jax.numpy as jnp
import numpy as np
from jax import lax

D = 400
NREL = 1024
ROUNDS = 2
SRC_DEV = 1024
BUCKET = 2048
SOURCES = 262144
DESTS = 16384
N_GRP = 8
N_WIDE = 32


def draw_src_rows(key, part):
    key_base = jax.random.fold_in(key, 11)
    normal_draw = jax.random.normal(key_base, (SOURCES, D), jnp.float32)
    values = jnp.clip(0.25 * normal_draw, -1.5, 1.5)
    return values.astype(jnp.bfloat16).astype(jnp.float32)


def draw_relations(key, part):
    key_base = jax.random.fold_in(key, 21)
    values = jnp.clip(jax.random.normal(key_base, (NREL, D), jnp.float32), -4.0, 4.0)
    return values.astype(jnp.bfloat16).astype(jnp.float32)


def touch_ends(array, key, least, top_value):
    extent = array.shape
    spot = [jax.random.randint(jax.random.fold_in(key, axis), (), 0, extent[axis]) for axis in range(len(extent))]
    array = array.at[tuple(spot)].set(least)
    longest = extent.index(max(extent))
    spot[longest] = (spot[longest] + 1) % extent[longest]
    return array.at[tuple(spot)].set(top_value)


def block_scale(rng, shape, cuts, least, largest):
    factor_of = 1.0
    for axis_at, blocks in cuts:
        draws = jax.random.uniform(jax.random.fold_in(jax.random.fold_in(rng, 6), axis_at), (blocks,), jnp.float32, least / len(cuts), largest / len(cuts))
        factor_of = factor_of * jnp.repeat(jnp.exp(draws), shape[axis_at] // blocks).reshape((-1,) + (1,) * (len(shape) - 1 - axis_at))
    return factor_of


def rank_bounds(count, lean):
    weights = [(1 << 20) // math.isqrt(grade ** lean) + 1 for grade in range(1, count + 1)]
    spread = 1 + sum(weights) // (1 << 30)
    return np.cumsum(np.array([max(1, weight // spread) for weight in weights]))


def ranked_ids(key, extent, number_of, slope):
    listing = rank_bounds(number_of, slope)
    pick = jax.random.randint(jax.random.fold_in(key, 1), extent, 0, int(listing[number_of - 1]))
    rank = jnp.searchsorted(jnp.asarray(listing, jnp.int32), pick, side="right")
    return jax.random.permutation(jax.random.fold_in(key, 2), number_of)[rank].astype(jnp.int32)


def scatter_about(own_key, dims, deviation, most, cuts=(), dtype=jnp.bfloat16):
    values = deviation * jax.random.normal(own_key, dims, jnp.float32)
    if cuts:
        values = values * block_scale(own_key, dims, cuts, -0.22, 0.18)
    return jnp.clip(values, -most, most).astype(dtype)


def setup_inputs(seed: int = 0) -> dict:
    key_list = jax.random.split(jax.random.key(seed), 8)
    return {
        "src_rows": draw_src_rows(jax.random.fold_in(key_list[7], 71), 0),
        "src_accum": jnp.clip(jnp.exp(math.log(4.0) - 3.6888794 * jax.random.uniform(key_list[1], (SOURCES,), jnp.float32) ** block_scale(key_list[1], (SOURCES,), ((0, 256),), -0.2, 0.2)), 0.1, 4.0),
        "dst_rows": scatter_about(key_list[2], (DESTS, D), 0.25, 1.5, ((0, 256),), jnp.float32),
        "dst_accum": jnp.clip(jnp.exp(math.log(4.0) - 3.6888794 * jax.random.uniform(key_list[3], (DESTS,), jnp.float32) ** block_scale(key_list[3], (DESTS,), ((0, 256),), -0.2, 0.2)), 0.1, 4.0),
        "relations": draw_relations(jax.random.fold_in(key_list[7], 71), 0),
        "rel_ids": touch_ends(ranked_ids(key_list[5], (ROUNDS, SOURCES), NREL, 2), jax.random.fold_in(key_list[5], 3), 0, NREL - 1).astype(jnp.int32),
        "targets": touch_ends(jax.random.randint(key_list[6], (ROUNDS, SOURCES), 0, BUCKET), jax.random.fold_in(key_list[6], 1), 0, BUCKET - 1).astype(jnp.int32),
    }


LEARN_RATE = 0.1

def adagrad(table_rows, accumulator, gradients):
    accumulator = accumulator + lax.optimization_barrier(jnp.mean(gradients * gradients, axis=-1))
    return (table_rows - LEARN_RATE * gradients / jnp.sqrt(accumulator)[..., None], accumulator)

def reference(src_rows, src_accum, dst_rows, dst_accum, relations, rel_ids, targets):
    group_count = SRC_DEV * N_WIDE
    block_rows = 512 if SRC_DEV % 512 == 0 else SRC_DEV
    block_count = SRC_DEV // block_rows

    def group_round(inputs):
        source_rows, source_accum, bucket_rows, id_list, label_ids = inputs
        key_rows = bucket_rows.astype(jnp.bfloat16).astype(jnp.float32)
        rel_scales = jnp.take(relations, id_list, axis=0)
        query_rows = (source_rows * rel_scales).astype(jnp.bfloat16)

        def visit(running, pieces):
            query, labels = pieces
            query_wide = query.astype(jnp.float32)
            logits = jnp.einsum('sd,bd->sb', query_wide, key_rows)
            top_score = lax.optimization_barrier(jnp.max(logits, axis=1, keepdims=True))
            exp_scores = jnp.exp(logits - top_score)
            exp_total = lax.optimization_barrier(jnp.sum(exp_scores, axis=1, keepdims=True))
            target_hit = lax.broadcasted_iota(jnp.int32, logits.shape, 1) == labels[:, None]
            picked = lax.optimization_barrier(jnp.sum(jnp.where(target_hit, logits, 0.0), axis=1))
            losses = top_score[:, 0] + jnp.log(exp_total[:, 0]) - picked
            residual = (exp_scores / exp_total - target_hit.astype(jnp.float32)).astype(jnp.bfloat16)
            residual_wide = residual.astype(jnp.float32)
            grad_query = jnp.einsum('sb,bd->sd', residual_wide, key_rows)
            running = running + jnp.einsum('sb,sd->bd', residual_wide, query_wide)
            return (running, (losses, grad_query))

        def one_slice(total, pieces):
            slice_query, slice_labels = pieces
            zeros = jnp.zeros((BUCKET, D), jnp.float32)
            partial_value, outputs = lax.scan(visit, zeros, (slice_query.reshape(block_count, block_rows, D), slice_labels.reshape(block_count, block_rows)))
            rounded = lax.optimization_barrier(partial_value.astype(jnp.bfloat16))
            return (total + rounded.astype(jnp.float32), outputs)
        grad_bucket, (losses, grad_query) = lax.scan(one_slice, jnp.zeros((BUCKET, D), jnp.float32), (query_rows.reshape(N_WIDE, SRC_DEV, D), label_ids.reshape(N_WIDE, SRC_DEV)))
        grad_source = grad_query.reshape(group_count, D) * rel_scales
        new_rows, new_accum = adagrad(source_rows, source_accum, grad_source)
        return (new_rows, new_accum, grad_bucket, losses.reshape(group_count))
    src_table = src_rows.reshape(N_GRP, group_count, D)
    src_acc = src_accum.reshape(N_GRP, group_count)
    held_rows = dst_rows.reshape(N_GRP, BUCKET, D)
    held_accum = dst_accum.reshape(N_GRP, BUCKET)
    loss_list = []
    for round_index in range(ROUNDS):
        ids_now = rel_ids[round_index].reshape(N_GRP, group_count)
        labels_now = targets[round_index].reshape(N_GRP, group_count)
        src_table, src_acc, grad_bucket, losses = lax.map(group_round, (src_table, src_acc, held_rows, ids_now, labels_now))
        held_rows, held_accum = adagrad(held_rows, held_accum, grad_bucket)
        loss_list.append(losses.reshape(N_GRP * group_count))
        if round_index + 1 < ROUNDS:
            held_rows = jnp.roll(held_rows, 1, axis=0)
            held_accum = jnp.roll(held_accum, 1, axis=0)
    return (src_table.reshape(N_GRP * group_count, D), src_acc.reshape(N_GRP * group_count), held_rows.reshape(N_GRP * BUCKET, D), held_accum.reshape(N_GRP * BUCKET), jnp.stack(loss_list))
```

```python
import functools

import jax
import jax.numpy as jnp
from jax import lax
from jax.experimental import pallas as pl
from jax.experimental.pallas import tpu as pltpu
from jax.sharding import PartitionSpec as P

MESH = pl.DeviceIdType.MESH
F32, BF16, I32 = jnp.float32, jnp.bfloat16, jnp.int32
LEARN_RATE = 0.1
D, DP = 400, 512
SRC, BUCKET, SHARD = 1024, 2048, 64
NZ, CHIPS = 8, 16
FLOWS = ((0, 1, 4), (1, -1, 4), (0, -1, 3), (1, 1, 3))
NEED = (4, -4, 3, -3, 2, -2, 1, -1, 0)


def place():
    g, w = lax.axis_index("grp"), lax.axis_index("wide")
    core = lax.rem(w, 2)
    z = lax.rem(lax.div(w, 2), NZ)
    y = lax.div(w, 2 * NZ)
    return g, y, z, core


def wide_of(y, z, core):
    return (y * NZ + z) * 2 + core


def wrap(z):
    return lax.rem(z + 2 * NZ, NZ)


def neighbours(y, z, core):
    return (
        wide_of(1 - y, z, core),
        wide_of(y, z, 1 - core),
        wide_of(y, wrap(z + 1), core),
        wide_of(y, wrap(z - 1), core),
    )


def greet(g, y, z, core, shift=False):
    barrier = pltpu.get_barrier_semaphore()
    targets = [(g, w) for w in neighbours(y, z, core)]
    if shift:
        me = wide_of(y, z, core)
        n = lax.axis_size("grp")
        targets += [(lax.rem(g + 1, n), me), (lax.rem(g + n - 1, n), me)]
    for target in targets:
        pl.semaphore_signal(barrier, inc=1, device_id=target, device_id_type=MESH)
    pl.semaphore_wait(barrier, len(targets))


def remote(src, dst, send, recv, target):
    return pltpu.make_async_remote_copy(
        src_ref=src, dst_ref=dst, send_sem=send, recv_sem=recv,
        device_id=target, device_id_type=MESH,
    )


def gather_keys(keys, ring_s, ring_r, pair_s, pair_r, g, y, z, core):
    yw, cw, rw, lw = neighbours(y, z, core)
    sent = []

    def push(slot, send, recv, w):
        copy = remote(keys.at[slot], keys.at[slot], send, recv, (g, w))
        copy.start()
        sent.append(copy)

    def landed(slot, send, recv, w):
        remote(keys.at[slot], keys.at[slot], send, recv, (g, w)).wait_recv()

    own = wide_of(y, z, core)
    other = wide_of(1 - y, z, core)
    push(own, ring_s.at[16], ring_r.at[16], yw)
    for f, (col, way, hops) in enumerate(FLOWS):
        if col == 0:
            push(own, ring_s.at[4 * f], ring_r.at[4 * f], rw if way > 0 else lw)
    push(own, pair_s.at[0], pair_r.at[0], cw)
    landed(other, ring_s.at[16], ring_r.at[16], yw)
    for f, (col, way, hops) in enumerate(FLOWS):
        if col == 1:
            push(other, ring_s.at[4 * f], ring_r.at[4 * f], rw if way > 0 else lw)
    push(other, pair_s.at[1], pair_r.at[1], cw)
    count = 2
    for k in range(4):
        for f, (col, way, hops) in enumerate(FLOWS):
            if k >= hops:
                continue
            column = y if col == 0 else 1 - y
            slot = wide_of(column, wrap(z - way * (k + 1)), core)
            landed(slot, ring_s.at[4 * f + k], ring_r.at[4 * f + k], lw)
            if k + 1 < hops:
                push(slot, ring_s.at[4 * f + k + 1], ring_r.at[4 * f + k + 1], rw if way > 0 else lw)
            push(slot, pair_s.at[count], pair_r.at[count], cw)
            count += 1
    landed(wide_of(y, z, 1 - core), pair_s.at[0], pair_r.at[0], cw)
    landed(wide_of(1 - y, z, 1 - core), pair_s.at[1], pair_r.at[1], cw)
    count = 2
    for k in range(4):
        for f, (col, way, hops) in enumerate(FLOWS):
            if k >= hops:
                continue
            column = y if col == 0 else 1 - y
            landed(wide_of(column, wrap(z - way * (k + 1)), 1 - core), pair_s.at[count], pair_r.at[count], cw)
            count += 1
    for copy in sent:
        copy.wait_send()


def scatter_sums(part, from_pair, out_sum, ring_in, ring_s, ring_r, pair_s, pair_r, g, y, z, core):
    yw, cw, rw, lw = neighbours(y, z, core)
    sent = []

    def chip(col, dz):
        return (y if col == 0 else 1 - y) * NZ + wrap(z + dz)

    order = []
    for k in range(4):
        for col, way, hops in FLOWS:
            if k < hops:
                order.append((col, way * (hops - k)))
    order += [(1, 0), (0, 0)]
    spot = {key: n for n, key in enumerate(order)}
    for n, (col, dz) in enumerate(order):
        q = chip(col, dz)
        copy = remote(part.at[1 - core, q], from_pair.at[q], pair_s.at[n], pair_r.at[n], (g, cw))
        copy.start()
        sent.append(copy)

    def mine(col, dz):
        q, n = chip(col, dz), spot[(col, dz)]
        remote(part.at[1 - core, q], from_pair.at[q], pair_s.at[n], pair_r.at[n], (g, cw)).wait_recv()
        return part[core, q].astype(F32) + from_pair[q].astype(F32)

    def arrived(f, k):
        remote(ring_in.at[4 * f + k], ring_in.at[4 * f + k], ring_s.at[4 * f + k], ring_r.at[4 * f + k], (g, lw)).wait_recv()
        return ring_in[4 * f + k].astype(F32)

    for k in range(4):
        for f, (col, way, hops) in enumerate(FLOWS):
            if k >= hops:
                continue
            total = mine(col, way * (hops - k))
            if k:
                total = total + arrived(f, k - 1)
            out_sum[4 * f + k] = total.astype(BF16)
            copy = remote(out_sum.at[4 * f + k], ring_in.at[4 * f + k], ring_s.at[4 * f + k], ring_r.at[4 * f + k], (g, rw if way > 0 else lw))
            copy.start()
            sent.append(copy)
    total = mine(1, 0) + arrived(1, 3) + arrived(3, 2)
    out_sum[16] = total.astype(BF16)
    copy = remote(out_sum.at[16], ring_in.at[16], ring_s.at[16], ring_r.at[16], (g, yw))
    copy.start()
    sent.append(copy)
    total = mine(0, 0) + arrived(0, 3) + arrived(2, 2)
    copy.wait_recv()
    total = total + ring_in[16].astype(F32)
    for copy in sent:
        copy.wait_send()
    return total


def column_of(row):
    n = row.shape[1]
    same = lax.broadcasted_iota(I32, (n, n), 0) == lax.broadcasted_iota(I32, (n, n), 1)
    return jnp.sum(jnp.where(same, row, 0.0), axis=1, keepdims=True)


def row_of(column):
    n = column.shape[0]
    same = lax.broadcasted_iota(I32, (n, n), 0) == lax.broadcasted_iota(I32, (n, n), 1)
    return jnp.sum(jnp.where(same, column, 0.0), axis=0, keepdims=True)


def adagrad_rows(rows, accum, grad):
    accum = accum + jnp.sum(grad * grad, axis=1, keepdims=True) * (1.0 / D)
    return rows - (LEARN_RATE * grad) / jnp.sqrt(accum), accum


def first_kernel(rows, keys, ring_s, ring_r, pair_s, pair_r):
    g, y, z, core = place()
    own = wide_of(y, z, core)
    keys[own] = jnp.zeros((SHARD, DP), BF16)
    keys[own, :, 0:D] = rows[...].astype(BF16)
    greet(g, y, z, core)
    gather_keys(keys, ring_s, ring_r, pair_s, pair_r, g, y, z, core)


def middle_kernel(part, rows, accum, keys, new_rows, new_accum,
                  from_pair, out_sum, ring_in, moved, landing,
                  ring_s, ring_r, pair_s, pair_r, ring_s2, ring_r2, pair_s2, pair_r2, move_s, move_r):
    g, y, z, core = place()
    own = wide_of(y, z, core)
    n = lax.axis_size("grp")
    greet(g, y, z, core, shift=True)
    grad = scatter_sums(part, from_pair, out_sum, ring_in, ring_s, ring_r, pair_s, pair_r, g, y, z, core)[:, 0:D]
    updated, total = adagrad_rows(rows[...], column_of(accum[...]), grad)
    moved[:, 384:512] = jnp.broadcast_to(total, (SHARD, 128))
    moved[:, 0:D] = updated
    copy = remote(moved, landing, move_s, move_r, (lax.rem(g + 1, n), own))
    copy.start()
    copy.wait()
    new_rows[...] = landing[:, 0:D]
    new_accum[...] = row_of(landing[:, D:D + 1])
    keys[own] = jnp.zeros((SHARD, DP), BF16)
    keys[own, :, 0:D] = landing[:, 0:D].astype(BF16)
    gather_keys(keys, ring_s2, ring_r2, pair_s2, pair_r2, g, y, z, core)


def last_kernel(part, rows, accum, new_rows, new_accum,
                from_pair, out_sum, ring_in, ring_s, ring_r, pair_s, pair_r):
    g, y, z, core = place()
    greet(g, y, z, core)
    grad = scatter_sums(part, from_pair, out_sum, ring_in, ring_s, ring_r, pair_s, pair_r, g, y, z, core)[:, 0:D]
    updated, total = adagrad_rows(rows[...], column_of(accum[...]), grad)
    new_rows[...] = updated
    new_accum[...] = row_of(total)


CHUNK = 512


def score_kernel(src, accum, rels, ids, labels, keys, new_src, new_accum, loss, part,
                 scale, query_t, query, logits, resid, keys_t):
    for t in range(4):
        lanes = slice(256 * t, 256 * t + 256)
        hot = (lax.broadcasted_iota(I32, (SRC, 256), 0) == ids[:, lanes]).astype(BF16)
        total = jnp.zeros((D, 256), F32)
        rest = rels[...]
        for _ in range(3):
            piece = rest.astype(BF16)
            rest = rest - piece.astype(F32)
            total = total + jnp.dot(piece, hot, preferred_element_type=F32)
        scale[:, lanes] = total
    query_t[D:DP] = jnp.zeros((DP - D, SRC), BF16)
    query_t[0:D] = (src[...] * scale[...]).astype(BF16)
    query[...] = query_t[...].T

    def score(j, top):
        at = pl.ds(pl.multiple_of(j * CHUNK, CHUNK), CHUNK)
        rows = keys[at]
        keys_t[:, at] = rows.T
        block = jnp.dot(rows, query_t[...], preferred_element_type=F32)
        logits[at] = block
        return jnp.maximum(top, jnp.max(block.reshape(CHUNK // 8, 8, SRC), axis=0))

    top = lax.fori_loop(0, BUCKET // CHUNK, score, jnp.full((8, SRC), -jnp.inf, F32))
    top = jnp.max(top, axis=0, keepdims=True)

    def weigh(j, sums):
        at = pl.ds(pl.multiple_of(j * CHUNK, CHUNK), CHUNK)
        block = logits[at]
        hit = lax.broadcasted_iota(I32, (CHUNK, SRC), 0) == labels[...] - j * CHUNK
        powers = jnp.exp(block - top)
        logits[at] = powers
        total, picked = sums
        total = total + jnp.sum(powers.reshape(CHUNK // 8, 8, SRC), axis=0)
        picked = picked + jnp.sum(jnp.where(hit, block, 0.0).reshape(CHUNK // 8, 8, SRC), axis=0)
        return total, picked

    zeros = jnp.zeros((8, SRC), F32)
    total, picked = lax.fori_loop(0, BUCKET // CHUNK, weigh, (zeros, zeros))
    total = jnp.sum(total, axis=0, keepdims=True)
    picked = jnp.sum(picked, axis=0, keepdims=True)
    loss[...] = top + jnp.log(total) - picked
    inverse = 1.0 / total

    def spread(j, _):
        at = pl.ds(pl.multiple_of(j * CHUNK, CHUNK), CHUNK)
        hit = lax.broadcasted_iota(I32, (CHUNK, SRC), 0) == labels[...] - j * CHUNK
        share = logits[at] * inverse
        block = jnp.where(hit, share - 1.0, share).astype(BF16)
        resid[at] = block
        grad = jnp.dot(block, query[...], preferred_element_type=F32).astype(BF16)
        chips = CHUNK // (2 * SHARD)
        for q in range(chips):
            for core in range(2):
                first = (2 * q + core) * SHARD
                part[core, j * chips + q] = grad[first:first + SHARD]
        return 0

    lax.fori_loop(0, BUCKET // CHUNK, spread, 0)
    for t in range(4):
        lanes = slice(256 * t, 256 * t + 256)
        grad = jnp.dot(keys_t[0:D], resid[:, lanes], preferred_element_type=F32) * scale[:, lanes]
        sums = accum[:, lanes] + jnp.sum(grad * grad, axis=0, keepdims=True) * (1.0 / D)
        new_accum[:, lanes] = sums
        new_src[:, lanes] = src[:, lanes] - (LEARN_RATE * grad) / jnp.sqrt(sums)


VM = pl.BlockSpec(memory_space=pltpu.VMEM)
DMA = pltpu.SemaphoreType.DMA
RING = [DMA((17,)), DMA((17,)), DMA((16,)), DMA((16,))]
BUFFERS = [
    pltpu.VMEM((CHIPS, SHARD, DP), BF16),
    pltpu.VMEM((17, SHARD, DP), BF16),
    pltpu.VMEM((17, SHARD, DP), BF16),
]


def call(body, shapes, inputs, scratch, collective=None, cost=None):
    return pl.pallas_call(
        body,
        out_shape=[jax.ShapeDtypeStruct(s, t) for s, t in shapes],
        in_specs=[VM] * inputs,
        out_specs=[VM] * len(shapes),
        scratch_shapes=scratch,
        compiler_params=pltpu.CompilerParams(
            collective_id=collective, has_side_effects=collective is not None,
            vmem_limit_bytes=60 * 1024 * 1024,
        ),
    )


def score(src, accum, rels, ids, labels, keys):
    return call(
        score_kernel,
        [((D, SRC), F32), ((1, SRC), F32), ((1, SRC), F32), ((2, CHIPS, SHARD, DP), BF16)],
        6,
        [
            pltpu.VMEM((D, SRC), F32), pltpu.VMEM((DP, SRC), BF16), pltpu.VMEM((SRC, DP), BF16),
            pltpu.VMEM((BUCKET, SRC), F32), pltpu.VMEM((BUCKET, SRC), BF16), pltpu.VMEM((DP, BUCKET), BF16),
        ],
    )(src, accum, rels, ids, labels, keys.reshape(BUCKET, DP))


def shards(src_rows, src_accum, dst_rows, dst_accum, relations, rel_ids, targets):
    src, rels = src_rows.T, relations.T
    accum = src_accum.reshape(1, SRC)
    (keys,) = call(first_kernel, [((32, SHARD, DP), BF16)], 1, RING, 0)(dst_rows)
    src, accum, loss0, part = score(src, accum, rels, rel_ids[0:1], targets[0:1], keys)
    keys, dst_rows, dst_accum = call(
        middle_kernel,
        [((32, SHARD, DP), BF16), ((SHARD, D), F32), ((1, SHARD), F32)],
        3,
        BUFFERS + [pltpu.VMEM((SHARD, DP), F32)] * 2 + RING + RING + [DMA(()), DMA(())],
        1,
    )(part, dst_rows, dst_accum.reshape(1, SHARD))
    src, accum, loss1, part = score(src, accum, rels, rel_ids[1:2], targets[1:2], keys)
    dst_rows, dst_accum = call(
        last_kernel, [((SHARD, D), F32), ((1, SHARD), F32)], 3, BUFFERS + RING, 2
    )(part, dst_rows, dst_accum)
    return (src.T, accum.reshape(SRC), dst_rows, dst_accum.reshape(SHARD), jnp.concatenate([loss0, loss1], axis=0))


def solution(mesh):
    both = ("grp", "wide")
    placed = (P(both, None), P(both), P(both, None), P(both), P(), P(None, both), P(None, both))
    return jax.shard_map(
        shards, mesh=mesh, in_specs=placed,
        out_specs=(P(both, None), P(both), P(both, None), P(both), P(None, both)),
        check_vma=False,
    )
```

```python
import jax
import jax.numpy as jnp
from jax import lax
from jax.experimental import pallas as pl
from jax.experimental.pallas import tpu as pltpu
from jax.sharding import PartitionSpec as P

MESH = pl.DeviceIdType.MESH
F32, BF16, I32 = jnp.float32, jnp.bfloat16, jnp.int32
LEARN_RATE = 0.1
D, DP = 400, 512
SRC, BUCKET, SHARD = 1024, 2048, 64
NZ, CHIPS = 8, 16
BLOCKS = (
    (1, -4), (1, 3), (1, -3), (1, 2),
    (0, 4), (0, -3), (0, 3), (0, -2),
    (1, -2), (1, 1), (1, -1), (1, 0),
    (0, 2), (0, -1), (0, 1), (0, 0),
)
SPOT = {(col, dz % NZ): p for p, (col, dz) in enumerate(BLOCKS)}
GROUP = 512
FLOWS = {0: ((1, 4), (-1, 3)), 1: ((-1, 4), (1, 3))}


def spot(col, dz):
    return SPOT[(col, dz % NZ)]


def ring_at(col, f, k):
    return (2 * col + f) * 4 + k


def place():
    g, w = lax.axis_index("grp"), lax.axis_index("wide")
    core = lax.rem(w, 2)
    z = lax.rem(lax.div(w, 2), NZ)
    y = lax.div(w, 2 * NZ)
    return g, y, z, core


def wide_of(y, z, core):
    return (y * NZ + z) * 2 + core


def wrap(z):
    return lax.rem(z + 2 * NZ, NZ)


def neighbours(y, z, core):
    return (
        wide_of(1 - y, z, core),
        wide_of(y, z, 1 - core),
        wide_of(y, wrap(z + 1), core),
        wide_of(y, wrap(z - 1), core),
    )


def greet(g, y, z, core, shift=False):
    barrier = pltpu.get_barrier_semaphore()
    targets = [(g, w) for w in neighbours(y, z, core)]
    if shift:
        me = wide_of(y, z, core)
        n = lax.axis_size("grp")
        targets += [(lax.rem(g + 1, n), me), (lax.rem(g + n - 1, n), me)]
    for target in targets:
        pl.semaphore_signal(barrier, inc=1, device_id=target, device_id_type=MESH)
    pl.semaphore_wait(barrier, len(targets))


def remote(src, dst, send, recv, target):
    return pltpu.make_async_remote_copy(
        src_ref=src, dst_ref=dst, send_sem=send, recv_sem=recv,
        device_id=target, device_id_type=MESH,
    )


class Gather:
    def __init__(self, keys, ring_s, ring_r, pair_s, pair_r, me):
        self.keys, self.sems, self.me, self.sent = keys, (ring_s, ring_r, pair_s, pair_r), me, []

    def copy(self, p, q, n, pair, w):
        g, y, z, core = self.me
        send, recv = self.sems[2:] if pair else self.sems[:2]
        return remote(self.keys.at[2 * p + core], self.keys.at[2 * q + core], send.at[n], recv.at[n], (g, w))

    def push(self, p, q, n, pair, w):
        copy = self.copy(p, q, n, pair, w)
        copy.start()
        self.sent.append(copy)

    def along(self, col, k, p_of):
        g, y, z, core = self.me
        yw, cw, rw, lw = neighbours(y, z, core)
        for f, (way, hops) in enumerate(FLOWS[col]):
            if k < hops:
                self.push(p_of(f, way, k), spot(col, -way * (k + 1)), ring_at(col, f, k), False, rw if way > 0 else lw)

    def start(self):
        g, y, z, core = self.me
        yw, cw, rw, lw = neighbours(y, z, core)
        own = spot(0, 0)
        self.push(own, spot(1, 0), 16, False, yw)
        self.along(0, 0, lambda f, way, k: own)
        self.push(own, own, own, True, cw)

    def across(self):
        g, y, z, core = self.me
        yw, cw, rw, lw = neighbours(y, z, core)
        other = spot(1, 0)
        self.copy(spot(0, 0), other, 16, False, yw).wait_recv()
        self.along(1, 0, lambda f, way, k: other)
        self.push(other, other, other, True, cw)

    def hop(self, col, k):
        g, y, z, core = self.me
        yw, cw, rw, lw = neighbours(y, z, core)
        for f, (way, hops) in enumerate(FLOWS[col]):
            if k >= hops:
                continue
            p = spot(col, -way * (k + 1))
            self.copy(p, p, ring_at(col, f, k), False, lw).wait_recv()
            if k + 1 < hops:
                self.push(p, spot(col, -way * (k + 2)), ring_at(col, f, k + 1), False, rw if way > 0 else lw)
            self.push(p, p, p, True, cw)

    def pair(self, group):
        g, y, z, core = self.me
        yw, cw, rw, lw = neighbours(y, z, core)
        for p in range(4 * group, 4 * group + 4):
            send, recv = self.sems[2:]
            slot = self.keys.at[2 * p + 1 - core]
            remote(slot, slot, send.at[p], recv.at[p], (g, cw)).wait_recv()

    def finish(self):
        for copy in self.sent:
            copy.wait_send()


class Scatter:
    def __init__(self, part, from_pair, out_sum, ring_in, ring_s, ring_r, pair_s, pair_r, me):
        self.part, self.from_pair, self.out_sum, self.ring_in = part, from_pair, out_sum, ring_in
        self.sems, self.me, self.sent = (ring_s, ring_r, pair_s, pair_r), me, []

    def swap(self, p):
        g, y, z, core = self.me
        yw, cw, rw, lw = neighbours(y, z, core)
        return remote(self.part.at[p, 1 - core], self.from_pair.at[p], self.sems[2].at[p], self.sems[3].at[p], (g, cw))

    def pair(self, group):
        for p in range(4 * group, 4 * group + 4):
            copy = self.swap(p)
            copy.start()
            self.sent.append(copy)

    def mine(self, col, dz):
        p = spot(col, dz)
        self.swap(p).wait_recv()
        return self.part[p, self.me[3]].astype(F32) + self.from_pair[p].astype(F32)

    def step(self, n, w):
        return remote(self.out_sum.at[n], self.ring_in.at[n], self.sems[0].at[n], self.sems[1].at[n], (self.me[0], w))

    def arrived(self, n):
        g, y, z, core = self.me
        self.step(n, neighbours(y, z, core)[3]).wait_recv()
        return self.ring_in[n].astype(F32)

    def send(self, n, total, w):
        self.out_sum[n] = total.astype(BF16)
        copy = self.step(n, w)
        copy.start()
        self.sent.append(copy)

    def hop(self, col, k):
        g, y, z, core = self.me
        yw, cw, rw, lw = neighbours(y, z, core)
        for f, (way, hops) in enumerate(FLOWS[col]):
            if k >= hops:
                continue
            total = self.mine(col, way * (hops - k))
            if k:
                total = total + self.arrived(ring_at(col, f, k - 1))
            self.send(ring_at(col, f, k), total, rw if way > 0 else lw)

    def last(self, col):
        total = self.mine(col, 0)
        for f, (way, hops) in enumerate(FLOWS[col]):
            total = total + self.arrived(ring_at(col, f, hops - 1))
        return total

    def across(self):
        g, y, z, core = self.me
        self.send(16, self.last(1), neighbours(y, z, core)[0])

    def finish(self):
        total = self.last(0)
        total = total + self.arrived(16)
        for copy in self.sent:
            copy.wait_send()
        return total


def column_of(row):
    n = row.shape[1]
    same = lax.broadcasted_iota(I32, (n, n), 0) == lax.broadcasted_iota(I32, (n, n), 1)
    return jnp.sum(jnp.where(same, row, 0.0), axis=1, keepdims=True)


def row_of(column):
    n = column.shape[0]
    same = lax.broadcasted_iota(I32, (n, n), 0) == lax.broadcasted_iota(I32, (n, n), 1)
    return jnp.sum(jnp.where(same, column, 0.0), axis=0, keepdims=True)


def adagrad_rows(rows, accum, grad):
    accum = accum + jnp.sum(grad * grad, axis=1, keepdims=True) * (1.0 / D)
    return rows - (LEARN_RATE * grad) / jnp.sqrt(accum), accum


def train_kernel(src, accum, rows, row_accum, rels, ids, labels,
                 new_src, new_accum, new_rows, new_row_accum, loss,
                 scale, query_t, query, logits, resid, keys_t,
                 keys0, keys1, part0, part1, pair0, pair1, out0, out1, in0, in1, key_row, moved, landing, tops,
                 *sems):
    me = g, y, z, core = place()
    here = wide_of(y, z, core)
    beyond = (lax.rem(g + 1, lax.axis_size("grp")), here)
    own = 2 * spot(0, 0) + core

    def tile(t):
        return slice(256 * t, 256 * t + 256)

    def relate(r, t):
        hot = (lax.broadcasted_iota(I32, (SRC, 256), 0) == ids[r:r + 1, tile(t)]).astype(BF16)
        total = jnp.zeros((D, 256), F32)
        rest = rels[...]
        for _ in range(3):
            piece = rest.astype(BF16)
            rest = rest - piece.astype(F32)
            total = total + jnp.dot(piece, hot, preferred_element_type=F32)
        scale[r, :, tile(t)] = total

    def ask(r, t):
        table = src if r == 0 else new_src
        quarter = (table[:, tile(t)] * scale[r, :, tile(t)]).astype(BF16)
        query_t[0:D, tile(t)] = quarter
        query[tile(t), 0:D] = quarter.T

    def hits(r, p):
        col, dz = BLOCKS[p]
        chip = (y if col == 0 else 1 - y) * NZ + wrap(z + dz)
        return lax.broadcasted_iota(I32, (128, SRC), 0) == labels[r:r + 1, :] - 128 * chip

    def fold(x):
        return x.reshape(-1, 8, SRC)

    class Softmax:
        def __init__(self, r, keys):
            self.r, self.keys, self.top = r, keys, None
            self.total = self.picked = None

        def score(self, group):
            rows_ = self.keys[8 * group:8 * group + 8].reshape(GROUP, DP)
            keys_t[:, GROUP * group:GROUP * group + GROUP] = rows_.T
            at = slice(GROUP * group, GROUP * group + GROUP)
            logits[at] = jnp.dot(rows_, query_t[...], preferred_element_type=F32)
            top = jnp.max(jnp.max(fold(logits[at]), axis=0), axis=0, keepdims=True)
            if self.top is not None:
                top = jnp.maximum(top, self.top)
            total = picked = jnp.zeros((8, SRC), F32)
            for p in range(4 * group, 4 * group + 4):
                lines = slice(128 * p, 128 * p + 128)
                block = logits[lines]
                powers = jnp.exp(block - top)
                picked = picked + jnp.sum(fold(jnp.where(hits(self.r, p), block, 0.0)), axis=0)
                total = total + jnp.sum(fold(powers), axis=0)
                logits[lines] = powers
            if self.top is not None:
                total = total + self.total * jnp.exp(self.top - top)
                picked = picked + self.picked
            self.top, self.total, self.picked = top, total, picked
            tops[group:group + 1] = top

        def close(self):
            total = jnp.sum(self.total, axis=0, keepdims=True)
            loss[self.r:self.r + 1] = self.top + jnp.log(total) - jnp.sum(self.picked, axis=0, keepdims=True)
            self.inverse = 1.0 / total

        def spread(self, group, part):
            factor = jnp.exp(tops[group:group + 1] - self.top) * self.inverse
            for p in range(4 * group, 4 * group + 4):
                lines = slice(128 * p, 128 * p + 128)
                share = logits[lines] * factor
                resid[lines] = jnp.where(hits(self.r, p), share - 1.0, share).astype(BF16)
            at = slice(GROUP * group, GROUP * group + GROUP)
            grad = jnp.dot(resid[at], query[...], preferred_element_type=F32).astype(BF16)
            part[4 * group:4 * group + 4] = grad.reshape(4, 2, SHARD, DP)

    def learn(r, t):
        table, totals = (src, accum) if r == 0 else (new_src, new_accum)
        grad = jnp.dot(keys_t[0:D], resid[:, tile(t)], preferred_element_type=F32) * scale[r, :, tile(t)]
        sums = totals[:, tile(t)] + jnp.sum(grad * grad, axis=0, keepdims=True) * (1.0 / D)
        new_accum[:, tile(t)] = sums
        new_src[:, tile(t)] = table[:, tile(t)] - (LEARN_RATE * grad) / jnp.sqrt(sums)

    keys0[own] = jnp.zeros((SHARD, DP), BF16)
    keys0[own, :, 0:D] = rows[...].astype(BF16)
    key_row[...] = jnp.zeros((SHARD, DP), BF16)
    query_t[D:DP] = jnp.zeros((DP - D, SRC), BF16)
    query[:, 384:DP] = jnp.zeros((SRC, DP - 384), BF16)
    greet(g, y, z, core, shift=True)
    gather = Gather(keys0, *sems[0:4], me)
    gather.start()
    relate(0, 0)
    gather.hop(0, 0)
    relate(0, 1)
    gather.across()
    relate(0, 2)
    gather.hop(0, 1)
    relate(0, 3)
    gather.hop(1, 0)
    ask(0, 0)
    ask(0, 1)
    gather.hop(0, 2)
    ask(0, 2)
    ask(0, 3)
    soft = Softmax(0, keys0)

    def rest_of_gather(gather, soft):
        gather.hop(1, 1)
        gather.pair(3)
        soft.score(3)
        gather.hop(0, 3)
        gather.hop(1, 2)
        gather.pair(2)
        soft.score(2)
        gather.hop(1, 3)
        gather.pair(1)
        soft.score(1)
        gather.pair(0)
        soft.score(0)
        soft.close()
        gather.finish()

    rest_of_gather(gather, soft)

    def rest_of_scatter(scatter, soft, part, r):
        soft.spread(0, part)
        scatter.pair(0)
        soft.spread(1, part)
        scatter.pair(1)
        scatter.hop(1, 0)
        soft.spread(2, part)
        scatter.pair(2)
        scatter.hop(0, 0)
        scatter.hop(1, 1)
        soft.spread(3, part)
        scatter.pair(3)
        scatter.hop(0, 1)
        scatter.hop(1, 2)
        learn(r, 0)
        scatter.hop(0, 2)
        scatter.hop(1, 3)
        learn(r, 1)
        scatter.across()
        scatter.hop(0, 3)
        learn(r, 2)
        learn(r, 3)

    scatter = Scatter(part0, pair0, out0, in0, *sems[4:8], me)
    rest_of_scatter(scatter, soft, part0, 0)
    grad = scatter.finish()[:, 0:D]
    updated, total = adagrad_rows(rows[...], column_of(row_accum[...]), grad)
    key_row[:, 0:D] = updated.astype(BF16)
    moved[:, 384:512] = jnp.broadcast_to(total, (SHARD, 128))
    moved[:, 0:D] = updated
    shift = remote(key_row, keys1.at[own], sems[16].at[0], sems[17].at[0], beyond)
    shift.start()
    carry = remote(moved, landing, sems[16].at[1], sems[17].at[1], beyond)
    carry.start()
    relate(1, 0)
    shift.wait_recv()
    gather = Gather(keys1, *sems[8:12], me)
    gather.start()
    relate(1, 1)
    gather.hop(0, 0)
    relate(1, 2)
    gather.across()
    relate(1, 3)
    gather.hop(0, 1)
    ask(1, 0)
    ask(1, 1)
    gather.hop(1, 0)
    gather.hop(0, 2)
    ask(1, 2)
    ask(1, 3)
    soft = Softmax(1, keys1)
    rest_of_gather(gather, soft)
    scatter = Scatter(part1, pair1, out1, in1, *sems[12:16], me)
    rest_of_scatter(scatter, soft, part1, 1)
    grad = scatter.finish()[:, 0:D]
    carry.wait_recv()
    updated, total = adagrad_rows(landing[:, 0:D], landing[:, D:D + 1], grad)
    new_rows[...] = updated
    new_row_accum[...] = row_of(total)
    shift.wait_send()
    carry.wait_send()


VM = pl.BlockSpec(memory_space=pltpu.VMEM)
DMA = pltpu.SemaphoreType.DMA


def shards(src_rows, src_accum, dst_rows, dst_accum, relations, rel_ids, targets):
    twice = lambda shape, kind: [pltpu.VMEM(shape, kind)] * 2
    new_src, new_accum, new_rows, new_row_accum, loss = pl.pallas_call(
        train_kernel,
        out_shape=[
            jax.ShapeDtypeStruct(s, F32) for s in ((D, SRC), (1, SRC), (SHARD, D), (1, SHARD), (2, SRC))
        ],
        in_specs=[VM] * 7,
        out_specs=[VM] * 5,
        scratch_shapes=[
            pltpu.VMEM((2, D, SRC), F32), pltpu.VMEM((DP, SRC), BF16), pltpu.VMEM((SRC, DP), BF16),
            pltpu.VMEM((BUCKET, SRC), F32), pltpu.VMEM((BUCKET, SRC), BF16), pltpu.VMEM((DP, BUCKET), BF16),
            *twice((32, SHARD, DP), BF16), *twice((CHIPS, 2, SHARD, DP), BF16), *twice((CHIPS, SHARD, DP), BF16),
            *twice((17, SHARD, DP), BF16), *twice((17, SHARD, DP), BF16),
            pltpu.VMEM((SHARD, DP), BF16), *twice((SHARD, DP), F32), pltpu.VMEM((8, SRC), F32),
            *([DMA((17,)), DMA((17,)), DMA((16,)), DMA((16,))] * 4), DMA((2,)), DMA((2,)),
        ],
        compiler_params=pltpu.CompilerParams(
            collective_id=0, has_side_effects=True, vmem_limit_bytes=62 * 1024 * 1024,
        ),
    )(src_rows.T, src_accum.reshape(1, SRC), dst_rows, dst_accum.reshape(1, SHARD), relations.T, rel_ids, targets)
    return (new_src.T, new_accum.reshape(SRC), new_rows, new_row_accum.reshape(SHARD), loss)


def solution(mesh):
    both = ("grp", "wide")
    placed = (P(both, None), P(both), P(both, None), P(both), P(), P(None, both), P(None, both))
    return jax.shard_map(
        shards, mesh=mesh, in_specs=placed,
        out_specs=(P(both, None), P(both), P(both, None), P(both), P(None, both)),
        check_vma=False,
    )
```

```python
import jax
import jax.numpy as jnp
from jax import lax
from jax.experimental import pallas as pl
from jax.experimental.pallas import tpu as pltpu
from jax.sharding import PartitionSpec as P

MESH = pl.DeviceIdType.MESH
F32, BF16, I32 = jnp.float32, jnp.bfloat16, jnp.int32
LEARN_RATE = 0.1
D, DP = 400, 512
SRC, BUCKET, SHARD = 1024, 2048, 64
NZ, CHIPS = 8, 16
GROUPS = (
    ((1, 4), (0, 4)),
    ((1, 3), (1, -3), (0, 3), (0, -3)),
    ((1, 2), (1, -2), (0, 2), (0, -2)),
    ((0, 1), (0, -1), (1, 0), (0, 0), (1, 1), (1, -1)),
)
BLOCKS = sum(GROUPS, ())
SPOT = {(col, dz % NZ): p for p, (col, dz) in enumerate(BLOCKS)}
SPANS = tuple(range(sum(map(len, GROUPS[:n])), sum(map(len, GROUPS[:n + 1]))) for n in range(len(GROUPS)))
SLOT = 208
DIRECT = ((0, 2), (0, -2), (1, 2), (1, -2), (0, 1), (0, -1), (1, 0), (1, 1), (1, -1))
RELAYS = tuple((col, way, more) for col in (0, 1) for way in (1, -1) for more in (1, 2) if more == 1 or way == (1, -1)[col])
STEPS = len(DIRECT) + len(RELAYS) + 1
HOME = STEPS - 1


def spot(col, dz):
    return SPOT[(col, dz % NZ)]


def direct_at(col, dz):
    return DIRECT.index((col, dz))


def relay_at(col, way, more):
    return len(DIRECT) + RELAYS.index((col, way, more))


def pack(x):
    last = x[:, 384:512]
    tail = last[0:16]
    for q in range(1, 4):
        tail = tail + pltpu.roll(last[16 * q:16 * q + 16], 16 * q, 1)
    return jnp.concatenate([x[:, 0:128], x[:, 128:256], x[:, 256:384], tail], axis=0)


def unpack_tail(tail):
    keep = lax.broadcasted_iota(I32, (16, 128), 1) < 16
    parts = [tail] + [pltpu.roll(tail, 128 - 16 * q, 1) for q in range(1, 4)]
    return jnp.concatenate([jnp.where(keep, part, 0.0) for part in parts], axis=0)


def unpack(x):
    return jnp.concatenate([x[0:64], x[64:128], x[128:192], unpack_tail(x[192:208])], axis=1)


def place():
    g, w = lax.axis_index("grp"), lax.axis_index("wide")
    core = lax.rem(w, 2)
    z = lax.rem(lax.div(w, 2), NZ)
    y = lax.div(w, 2 * NZ)
    return g, y, z, core


def wide_of(y, z, core):
    return (y * NZ + z) * 2 + core


def wrap(z):
    return lax.rem(z + 2 * NZ, NZ)


def at(me, col, dz):
    g, y, z, core = me
    return wide_of(y if col == 0 else 1 - y, wrap(z + dz), core)


def greet(me):
    g, y, z, core = me
    n = lax.axis_size("grp")
    barrier = pltpu.get_barrier_semaphore()
    around = [at(me, col, dz) for col, dz in DIRECT]
    targets = [(g, w) for w in around + [wide_of(y, z, 1 - core)]]
    for other in (lax.rem(g + 1, n), lax.rem(g + n - 1, n)):
        targets.append((other, wide_of(y, z, core)))
    for target in targets:
        pl.semaphore_signal(barrier, inc=1, device_id=target, device_id_type=MESH)
    pl.semaphore_wait(barrier, len(targets))


def remote(src, dst, send, recv, target):
    return pltpu.make_async_remote_copy(
        src_ref=src, dst_ref=dst, send_sem=send, recv_sem=recv,
        device_id=target, device_id_type=MESH,
    )


class Gather:
    def __init__(self, keys, step_s, step_r, pair_s, pair_r, me):
        self.keys, self.sems, self.me, self.sent = keys, (step_s, step_r, pair_s, pair_r), me, []

    def copy(self, p, q, n, device, pair=False):
        core = self.me[3]
        send, recv = self.sems[2:] if pair else self.sems[:2]
        return remote(self.keys.at[2 * p + core], self.keys.at[2 * q + core], send.at[n], recv.at[n], device)

    def push(self, *args, **kwargs):
        copy = self.copy(*args, **kwargs)
        copy.start()
        self.sent.append(copy)

    def share(self, p):
        g, y, z, core = self.me
        self.push(p, p, p, (g, wide_of(y, z, 1 - core)), pair=True)

    def start(self):
        own = spot(0, 0)
        for col, dz in DIRECT:
            self.push(own, spot(col, -dz), direct_at(col, dz), (self.me[0], at(self.me, col, dz)))
        self.share(own)

    def wait(self, p, n):
        g, y, z, core = self.me
        self.copy(p, p, n, (g, wide_of(y, z, 1 - core))).wait_recv()

    def relay(self, col):
        for way in (1, -1):
            p = spot(col, -2 * way)
            self.wait(p, direct_at(col, 2 * way))
            for more in (2, 1):
                if (col, way, more) in RELAYS:
                    self.push(p, spot(col, -way * (2 + more)), relay_at(col, way, more), (self.me[0], at(self.me, 0, way * more)))
            self.share(p)

    def near(self, col, dz):
        p = spot(col, -dz)
        self.wait(p, direct_at(col, dz))
        self.share(p)

    def far(self, col, more):
        for way in (1, -1):
            if (col, way, more) in RELAYS:
                p = spot(col, -way * (2 + more))
                self.wait(p, relay_at(col, way, more))
                self.share(p)

    def pair(self, group):
        g, y, z, core = self.me
        for p in SPANS[group]:
            slot = self.keys.at[2 * p + 1 - core]
            remote(slot, slot, self.sems[2].at[p], self.sems[3].at[p], (g, wide_of(y, z, 1 - core))).wait_recv()

    def finish(self):
        for copy in self.sent:
            copy.wait_send()


class Scatter:
    def __init__(self, part, from_pair, out_sum, inbox, step_s, step_r, pair_s, pair_r, me):
        self.part, self.from_pair, self.out_sum, self.inbox = part, from_pair, out_sum, inbox
        self.sems, self.me, self.sent = (step_s, step_r, pair_s, pair_r), me, []

    def swap(self, p):
        g, y, z, core = self.me
        return remote(self.part.at[p, 1 - core], self.from_pair.at[p], self.sems[2].at[p], self.sems[3].at[p],
                      (g, wide_of(y, z, 1 - core)))

    def pair(self, group):
        for p in SPANS[group]:
            copy = self.swap(p)
            copy.start()
            self.sent.append(copy)

    def mine(self, col, dz):
        p = spot(col, dz)
        self.swap(p).wait_recv()
        return self.part[p, self.me[3]].astype(F32) + self.from_pair[p].astype(F32)

    def step(self, n, w):
        return remote(self.out_sum.at[n], self.inbox.at[n], self.sems[0].at[n], self.sems[1].at[n], (self.me[0], w))

    def arrived(self, n):
        self.step(n, at(self.me, 0, 1)).wait_recv()
        return self.inbox[n].astype(F32)

    def send(self, n, total, w):
        self.out_sum[n] = total.astype(BF16)
        copy = self.step(n, w)
        copy.start()
        self.sent.append(copy)

    def far(self, col, more):
        for way in (1, -1):
            if (col, way, more) in RELAYS:
                self.send(relay_at(col, way, more), self.mine(col, way * (2 + more)), at(self.me, 0, way * more))

    def relay(self, col):
        for way in (1, -1):
            total = self.mine(col, 2 * way)
            for more in (1, 2):
                if (col, way, more) in RELAYS:
                    total = total + self.arrived(relay_at(col, way, more))
            self.send(direct_at(col, 2 * way), total, at(self.me, col, 2 * way))

    def near(self, col, dz):
        self.send(direct_at(col, dz), self.mine(col, dz), at(self.me, col, dz))

    def finish(self):
        total = self.mine(0, 0)
        for col, dz in ((0, 1), (0, -1), (1, 0), (1, 1), (1, -1), (0, 2), (0, -2), (1, 2), (1, -2)):
            total = total + self.arrived(direct_at(col, dz))
        for copy in self.sent:
            copy.wait_send()
        return unpack(total)


def column_of(row):
    n = row.shape[1]
    same = lax.broadcasted_iota(I32, (n, n), 0) == lax.broadcasted_iota(I32, (n, n), 1)
    return jnp.sum(jnp.where(same, row, 0.0), axis=1, keepdims=True)


def row_of(column):
    n = column.shape[0]
    same = lax.broadcasted_iota(I32, (n, n), 0) == lax.broadcasted_iota(I32, (n, n), 1)
    return jnp.sum(jnp.where(same, column, 0.0), axis=0, keepdims=True)


def adagrad_rows(rows, accum, grad):
    accum = accum + jnp.sum(grad * grad, axis=1, keepdims=True) * (1.0 / D)
    return rows - (LEARN_RATE * grad) / jnp.sqrt(accum), accum


def train_kernel(src, accum, rows, row_accum, rels, ids, labels,
                 new_src, new_accum, new_rows, new_row_accum, loss,
                 scale, query_t, query, logits, resid, keys_t,
                 keys0, keys1, part0, part1, pair0, pair1, out0, out1, in0, in1, key_row, moved, landing, tops,
                 *sems):
    me = g, y, z, core = place()
    here = wide_of(y, z, core)
    beyond = (lax.rem(g + 1, lax.axis_size("grp")), here)
    own = 2 * spot(0, 0) + core

    def tile(t):
        return slice(256 * t, 256 * t + 256)

    def relate(r, t):
        hot = (lax.broadcasted_iota(I32, (SRC, 256), 0) == ids[r:r + 1, tile(t)]).astype(BF16)
        total = jnp.zeros((D, 256), F32)
        rest = rels[...]
        for _ in range(3):
            piece = rest.astype(BF16)
            rest = rest - piece.astype(F32)
            total = total + jnp.dot(piece, hot, preferred_element_type=F32)
        scale[r, :, tile(t)] = total

    def ask(r, t):
        table = src if r == 0 else new_src
        quarter = (table[:, tile(t)] * scale[r, :, tile(t)]).astype(BF16)
        query_t[0:D, tile(t)] = quarter
        query[tile(t), 0:D] = quarter.T

    def hits(r, p):
        col, dz = BLOCKS[p]
        chip = (y if col == 0 else 1 - y) * NZ + wrap(z + dz)
        return lax.broadcasted_iota(I32, (128, SRC), 0) == labels[r:r + 1, :] - 128 * chip

    def fold(x):
        return x.reshape(-1, 8, SRC)

    class Softmax:
        def __init__(self, r, keys):
            self.r, self.keys, self.top = r, keys, None
            self.total = self.picked = None

        def score(self, group):
            pieces = []
            for s in range(2 * SPANS[group][0], 2 * SPANS[group][-1] + 2):
                end = unpack_tail(self.keys[s, 192:208].astype(F32)).astype(BF16)
                pieces.append(jnp.concatenate([self.keys[s, 0:64], self.keys[s, 64:128], self.keys[s, 128:192], end], axis=1))
            rows_ = jnp.concatenate(pieces, axis=0)
            at = slice(128 * SPANS[group][0], 128 * SPANS[group][-1] + 128)
            keys_t[:, at] = rows_.T
            logits[at] = jnp.dot(rows_, query_t[...], preferred_element_type=F32)
            top = jnp.max(jnp.max(fold(logits[at]), axis=0), axis=0, keepdims=True)
            if self.top is not None:
                top = jnp.maximum(top, self.top)
            total = picked = jnp.zeros((8, SRC), F32)
            for p in SPANS[group]:
                lines = slice(128 * p, 128 * p + 128)
                block = logits[lines]
                powers = jnp.exp(block - top)
                picked = picked + jnp.sum(fold(jnp.where(hits(self.r, p), block, 0.0)), axis=0)
                total = total + jnp.sum(fold(powers), axis=0)
                logits[lines] = powers
            if self.top is not None:
                total = total + self.total * jnp.exp(self.top - top)
                picked = picked + self.picked
            self.top, self.total, self.picked = top, total, picked
            tops[group:group + 1] = top

        def close(self):
            total = jnp.sum(self.total, axis=0, keepdims=True)
            loss[self.r:self.r + 1] = self.top + jnp.log(total) - jnp.sum(self.picked, axis=0, keepdims=True)
            self.inverse = 1.0 / total

        def spread(self, group, part):
            factor = jnp.exp(tops[group:group + 1] - self.top) * self.inverse
            for p in SPANS[group]:
                lines = slice(128 * p, 128 * p + 128)
                share = logits[lines] * factor
                resid[lines] = jnp.where(hits(self.r, p), share - 1.0, share).astype(BF16)
            at = slice(128 * SPANS[group][0], 128 * SPANS[group][-1] + 128)
            grad = jnp.dot(resid[at], query[...], preferred_element_type=F32)
            for p in range(2 * len(SPANS[group])):
                part[SPANS[group][0] + p // 2, p % 2] = pack(grad[SHARD * p:SHARD * p + SHARD]).astype(BF16)

    def learn(r, t):
        table, totals = (src, accum) if r == 0 else (new_src, new_accum)
        grad = jnp.dot(keys_t[0:D], resid[:, tile(t)], preferred_element_type=F32) * scale[r, :, tile(t)]
        sums = totals[:, tile(t)] + jnp.sum(grad * grad, axis=0, keepdims=True) * (1.0 / D)
        new_accum[:, tile(t)] = sums
        new_src[:, tile(t)] = table[:, tile(t)] - (LEARN_RATE * grad) / jnp.sqrt(sums)

    def wide_rows(x):
        return jnp.concatenate([x, jnp.zeros((SHARD, DP - D), F32)], axis=1)

    keys0[own] = pack(wide_rows(rows[...])).astype(BF16)
    query_t[D:DP] = jnp.zeros((DP - D, SRC), BF16)
    query[:, 384:DP] = jnp.zeros((SRC, DP - 384), BF16)
    greet(me)
    gather = first_gather = Gather(keys0, *sems[0:4], me)
    gather.start()
    for t in range(3):
        relate(0, t)
        ask(0, t)
    gather.relay(0)
    gather.relay(1)
    relate(0, 3)
    ask(0, 3)
    soft = Softmax(0, keys0)

    def rest_of_gather(gather, soft):
        for col, dz in ((0, 1), (0, -1), (1, 0), (1, 1), (1, -1)):
            gather.near(col, dz)
        gather.pair(3)
        soft.score(3)
        gather.far(0, 1)
        gather.far(1, 1)
        gather.pair(2)
        soft.score(2)
        gather.far(0, 2)
        gather.far(1, 2)
        gather.pair(1)
        soft.score(1)
        gather.pair(0)
        soft.score(0)
        soft.close()

    rest_of_gather(gather, soft)

    def rest_of_scatter(scatter, soft, part, r):
        soft.spread(0, part)
        scatter.pair(0)
        soft.spread(1, part)
        scatter.pair(1)
        scatter.far(1, 2)
        scatter.far(0, 2)
        scatter.far(1, 1)
        scatter.far(0, 1)
        soft.spread(2, part)
        scatter.pair(2)
        soft.spread(3, part)
        scatter.pair(3)
        scatter.relay(1)
        scatter.relay(0)
        scatter.near(1, 1)
        scatter.near(1, -1)
        scatter.near(1, 0)
        scatter.near(0, 1)
        scatter.near(0, -1)
        for t in range(4):
            learn(r, t)

    scatter = Scatter(part0, pair0, out0, in0, *sems[4:8], me)
    rest_of_scatter(scatter, soft, part0, 0)
    grad = scatter.finish()[:, 0:D]
    updated, total = adagrad_rows(rows[...], column_of(row_accum[...]), grad)
    key_row[...] = pack(wide_rows(updated)).astype(BF16)
    shift = remote(key_row, keys1.at[own], sems[16].at[0], sems[17].at[0], beyond)
    shift.start()
    moved[...] = wide_rows(updated)
    moved[:, 384:512] = jnp.where(lax.broadcasted_iota(I32, (SHARD, 128), 1) < 16, moved[:, 384:512], total)
    carry = remote(moved, landing, sems[16].at[1], sems[17].at[1], beyond)
    carry.start()
    relate(1, 0)
    relate(1, 1)
    shift.wait_recv()
    gather = Gather(keys1, *sems[8:12], me)
    gather.start()
    relate(1, 2)
    relate(1, 3)
    ask(1, 0)
    ask(1, 1)
    gather.relay(0)
    gather.relay(1)
    ask(1, 2)
    ask(1, 3)
    soft = Softmax(1, keys1)
    rest_of_gather(gather, soft)
    scatter = Scatter(part1, pair1, out1, in1, *sems[12:16], me)
    rest_of_scatter(scatter, soft, part1, 1)
    grad = scatter.finish()[:, 0:D]
    carry.wait_recv()
    updated, total = adagrad_rows(landing[:, 0:D], landing[:, D:D + 1], grad)
    new_rows[...] = updated
    new_row_accum[...] = row_of(total)
    carry.wait_send()
    first_gather.finish()
    gather.finish()
    shift.wait_send()


VM = pl.BlockSpec(memory_space=pltpu.VMEM)
DMA = pltpu.SemaphoreType.DMA


def hand_over(*arrays):
    def kernel(*refs):
        half = len(refs) // 2
        for source, target in zip(refs[:half], refs[half:]):
            target[...] = source[...]

    return pl.pallas_call(
        kernel,
        out_shape=[jax.ShapeDtypeStruct(a.shape, a.dtype) for a in arrays],
        in_specs=[VM] * len(arrays),
        out_specs=[VM] * len(arrays),
    )(*arrays)


def shards(src_rows, src_accum, dst_rows, dst_accum, relations, rel_ids, targets):
    twice = lambda shape, kind: [pltpu.VMEM(shape, kind)] * 2
    new_src, new_accum, new_rows, new_row_accum, loss = pl.pallas_call(
        train_kernel,
        out_shape=[
            jax.ShapeDtypeStruct(s, F32) for s in ((D, SRC), (1, SRC), (SHARD, D), (1, SHARD), (2, SRC))
        ],
        in_specs=[VM] * 7,
        out_specs=[VM] * 5,
        scratch_shapes=[
            pltpu.VMEM((2, D, SRC), F32), pltpu.VMEM((DP, SRC), BF16), pltpu.VMEM((SRC, DP), BF16),
            pltpu.VMEM((BUCKET, SRC), F32), pltpu.VMEM((BUCKET, SRC), BF16), pltpu.VMEM((DP, BUCKET), BF16),
            *twice((32, SLOT, 128), BF16), *twice((CHIPS, 2, SLOT, 128), BF16), *twice((CHIPS, SLOT, 128), BF16),
            *twice((STEPS, SLOT, 128), BF16), *twice((STEPS, SLOT, 128), BF16),
            pltpu.VMEM((SLOT, 128), BF16), *twice((SHARD, DP), F32), pltpu.VMEM((8, SRC), F32),
            *([DMA((STEPS,)), DMA((STEPS,)), DMA((CHIPS,)), DMA((CHIPS,))] * 4), DMA((2,)), DMA((2,)),
        ],
        compiler_params=pltpu.CompilerParams(
            collective_id=0, has_side_effects=True, vmem_limit_bytes=62 * 1024 * 1024,
        ),
    )(src_rows.T, src_accum.reshape(1, SRC), dst_rows, dst_accum.reshape(1, SHARD), relations.T, rel_ids, targets)
    (new_src, new_accum, new_rows, new_row_accum, loss) = hand_over(new_src, new_accum, new_rows, new_row_accum, loss)
    return (new_src.T, new_accum.reshape(SRC), new_rows, new_row_accum.reshape(SHARD), loss)


def solution(mesh):
    both = ("grp", "wide")
    placed = (P(both, None), P(both), P(both, None), P(both), P(), P(None, both), P(None, both))
    return jax.shard_map(
        shards, mesh=mesh, in_specs=placed,
        out_specs=(P(both, None), P(both), P(both, None), P(both), P(None, both)),
        check_vma=False,
    )
```

```python
import jax
import jax.numpy as jnp
from jax import lax
from jax.experimental import pallas as pl
from jax.experimental.pallas import tpu as pltpu
from jax.sharding import PartitionSpec as P

MESH = pl.DeviceIdType.MESH
F32, BF16, I32 = jnp.float32, jnp.bfloat16, jnp.int32
LEARN_RATE = 0.1
D, DP = 400, 512
SRC, BUCKET, SHARD = 1024, 2048, 64
NZ, CHIPS = 8, 16
GROUPS = (
    ((1, 4), (0, 4)),
    ((1, 3), (1, -3), (0, 3), (0, -3)),
    ((0, 1), (0, -1), (1, 1), (1, -1)),
    ((1, 2), (1, -2), (0, 2), (0, -2), (1, 0), (0, 0)),
)
BLOCKS = sum(GROUPS, ())
SPOT = {(col, dz % NZ): p for p, (col, dz) in enumerate(BLOCKS)}
SPANS = tuple(range(sum(map(len, GROUPS[:n])), sum(map(len, GROUPS[:n + 1]))) for n in range(len(GROUPS)))
SLOT = 208
DIRECT = ((1, 2), (1, -2), (0, 2), (0, -2), (1, 0), (1, 1), (1, -1), (0, 1), (0, -1))
RELAYS = tuple((col, way, more) for col in (0, 1) for way in (1, -1) for more in (1, 2) if more == 1 or way == (1, -1)[col])
STEPS = len(DIRECT) + len(RELAYS) + 1
HOME = STEPS - 1


def spot(col, dz):
    return SPOT[(col, dz % NZ)]


def direct_at(col, dz):
    return DIRECT.index((col, dz))


def relay_at(col, way, more):
    return len(DIRECT) + RELAYS.index((col, way, more))


def pack(x):
    last = x[:, 384:512]
    tail = last[0:16]
    for q in range(1, 4):
        tail = tail + pltpu.roll(last[16 * q:16 * q + 16], 16 * q, 1)
    return jnp.concatenate([x[:, 0:128], x[:, 128:256], x[:, 256:384], tail], axis=0)


def unpack_tail(tail):
    keep = lax.broadcasted_iota(I32, (16, 128), 1) < 16
    parts = [tail] + [pltpu.roll(tail, 128 - 16 * q, 1) for q in range(1, 4)]
    return jnp.concatenate([jnp.where(keep, part, 0.0) for part in parts], axis=0)


def unpack(x):
    return jnp.concatenate([x[0:64], x[64:128], x[128:192], unpack_tail(x[192:208])], axis=1)


def place():
    g, w = lax.axis_index("grp"), lax.axis_index("wide")
    core = lax.rem(w, 2)
    z = lax.rem(lax.div(w, 2), NZ)
    y = lax.div(w, 2 * NZ)
    return g, y, z, core


def wide_of(y, z, core):
    return (y * NZ + z) * 2 + core


def wrap(z):
    return lax.rem(z + 2 * NZ, NZ)


def at(me, col, dz):
    g, y, z, core = me
    return wide_of(y if col == 0 else 1 - y, wrap(z + dz), core)


def greet(me):
    g, y, z, core = me
    n = lax.axis_size("grp")
    barrier = pltpu.get_barrier_semaphore()
    around = [at(me, col, dz) for col, dz in DIRECT]
    targets = [(g, w) for w in around + [wide_of(y, z, 1 - core)]]
    for other in (lax.rem(g + 1, n), lax.rem(g + n - 1, n)):
        targets.append((other, wide_of(y, z, core)))
    for target in targets:
        pl.semaphore_signal(barrier, inc=1, device_id=target, device_id_type=MESH)
    pl.semaphore_wait(barrier, len(targets))


def remote(src, dst, send, recv, target):
    return pltpu.make_async_remote_copy(
        src_ref=src, dst_ref=dst, send_sem=send, recv_sem=recv,
        device_id=target, device_id_type=MESH,
    )


class Gather:
    def __init__(self, keys, step_s, step_r, pair_s, pair_r, me):
        self.keys, self.sems, self.me, self.sent = keys, (step_s, step_r, pair_s, pair_r), me, []

    def copy(self, p, q, n, device, pair=False):
        core = self.me[3]
        send, recv = self.sems[2:] if pair else self.sems[:2]
        return remote(self.keys.at[2 * p + core], self.keys.at[2 * q + core], send.at[n], recv.at[n], device)

    def push(self, *args, **kwargs):
        copy = self.copy(*args, **kwargs)
        copy.start()
        self.sent.append(copy)

    def share(self, p):
        g, y, z, core = self.me
        self.push(p, p, p, (g, wide_of(y, z, 1 - core)), pair=True)

    def start(self):
        own = spot(0, 0)
        for col, dz in DIRECT:
            self.push(own, spot(col, -dz), direct_at(col, dz), (self.me[0], at(self.me, col, dz)))
        self.share(own)

    def wait(self, p, n):
        g, y, z, core = self.me
        self.copy(p, p, n, (g, wide_of(y, z, 1 - core))).wait_recv()

    def relay(self, col):
        for way in (1, -1):
            p = spot(col, -2 * way)
            self.wait(p, direct_at(col, 2 * way))
            for more in (2, 1):
                if (col, way, more) in RELAYS:
                    self.push(p, spot(col, -way * (2 + more)), relay_at(col, way, more), (self.me[0], at(self.me, 0, way * more)))
            self.share(p)

    def near(self, col, dz):
        p = spot(col, -dz)
        self.wait(p, direct_at(col, dz))
        self.share(p)

    def far(self, col, more):
        for way in (1, -1):
            if (col, way, more) in RELAYS:
                p = spot(col, -way * (2 + more))
                self.wait(p, relay_at(col, way, more))
                self.share(p)

    def pair(self, group):
        g, y, z, core = self.me
        for p in SPANS[group]:
            slot = self.keys.at[2 * p + 1 - core]
            remote(slot, slot, self.sems[2].at[p], self.sems[3].at[p], (g, wide_of(y, z, 1 - core))).wait_recv()

    def finish(self):
        for copy in self.sent:
            copy.wait_send()


class Scatter:
    def __init__(self, part, from_pair, out_sum, inbox, step_s, step_r, pair_s, pair_r, me):
        self.part, self.from_pair, self.out_sum, self.inbox = part, from_pair, out_sum, inbox
        self.sems, self.me, self.sent = (step_s, step_r, pair_s, pair_r), me, []

    def swap(self, p):
        g, y, z, core = self.me
        return remote(self.part.at[p, 1 - core], self.from_pair.at[p], self.sems[2].at[p], self.sems[3].at[p],
                      (g, wide_of(y, z, 1 - core)))

    def pair(self, group):
        for p in SPANS[group]:
            copy = self.swap(p)
            copy.start()
            self.sent.append(copy)

    def mine(self, col, dz):
        p = spot(col, dz)
        self.swap(p).wait_recv()
        return self.part[p, self.me[3]].astype(F32) + self.from_pair[p].astype(F32)

    def step(self, n, w):
        return remote(self.out_sum.at[n], self.inbox.at[n], self.sems[0].at[n], self.sems[1].at[n], (self.me[0], w))

    def arrived(self, n):
        self.step(n, at(self.me, 0, 1)).wait_recv()
        return self.inbox[n].astype(F32)

    def send(self, n, total, w):
        self.out_sum[n] = total.astype(BF16)
        copy = self.step(n, w)
        copy.start()
        self.sent.append(copy)

    def far(self, col, more):
        for way in (1, -1):
            if (col, way, more) in RELAYS:
                self.send(relay_at(col, way, more), self.mine(col, way * (2 + more)), at(self.me, 0, way * more))

    def relay(self, col):
        for way in (1, -1):
            total = self.mine(col, 2 * way)
            for more in (1, 2):
                if (col, way, more) in RELAYS:
                    total = total + self.arrived(relay_at(col, way, more))
            self.send(direct_at(col, 2 * way), total, at(self.me, col, 2 * way))

    def near(self, col, dz):
        self.send(direct_at(col, dz), self.mine(col, dz), at(self.me, col, dz))

    def finish(self):
        total = self.mine(0, 0)
        for col, dz in ((0, 1), (0, -1), (1, 0), (1, 1), (1, -1), (0, 2), (0, -2), (1, 2), (1, -2)):
            total = total + self.arrived(direct_at(col, dz))
        for copy in self.sent:
            copy.wait_send()
        return unpack(total)


def column_of(row):
    n = row.shape[1]
    same = lax.broadcasted_iota(I32, (n, n), 0) == lax.broadcasted_iota(I32, (n, n), 1)
    return jnp.sum(jnp.where(same, row, 0.0), axis=1, keepdims=True)


def row_of(column):
    n = column.shape[0]
    same = lax.broadcasted_iota(I32, (n, n), 0) == lax.broadcasted_iota(I32, (n, n), 1)
    return jnp.sum(jnp.where(same, column, 0.0), axis=0, keepdims=True)


def adagrad_rows(rows, accum, grad):
    accum = accum + jnp.sum(grad * grad, axis=1, keepdims=True) * (1.0 / D)
    return rows - (LEARN_RATE * grad) / jnp.sqrt(accum), accum


def train_kernel(src, accum, rows, row_accum, rels, ids, labels,
                 new_src, new_accum, new_rows, new_row_accum, loss,
                 scale, query_t, query, logits, resid, keys_t, key_rows,
                 keys0, keys1, part0, part1, pair0, pair1, out0, out1, in0, in1, key_row, moved, landing, tops,
                 *sems):
    me = g, y, z, core = place()
    here = wide_of(y, z, core)
    beyond = (lax.rem(g + 1, lax.axis_size("grp")), here)
    own = 2 * spot(0, 0) + core

    def tile(t):
        return slice(256 * t, 256 * t + 256)

    def relate(r, t):
        hot = (lax.broadcasted_iota(I32, (SRC, 256), 0) == ids[r:r + 1, tile(t)]).astype(BF16)
        total = jnp.zeros((D, 256), F32)
        rest = rels[...]
        for _ in range(3):
            piece = rest.astype(BF16)
            rest = rest - piece.astype(F32)
            total = total + jnp.dot(piece, hot, preferred_element_type=F32)
        scale[r, :, tile(t)] = total

    def ask(r, t):
        table = src if r == 0 else new_src
        quarter = (table[:, tile(t)] * scale[r, :, tile(t)]).astype(BF16)
        query_t[0:D, tile(t)] = quarter
        query[tile(t), 0:D] = quarter.T

    def hits(r, p, t):
        col, dz = BLOCKS[p]
        chip = (y if col == 0 else 1 - y) * NZ + wrap(z + dz)
        return lax.broadcasted_iota(I32, (128, 256), 0) == labels[r:r + 1, tile(t)] - 128 * chip

    def fold(x):
        return x.reshape(-1, 8, x.shape[1])

    class Softmax:
        def __init__(self, r, keys):
            self.r, self.keys = r, keys
            self.top, self.total, self.picked = [None] * 4, [None] * 4, [None] * 4

        def score(self, group):
            pieces = []
            for s in range(2 * SPANS[group][0], 2 * SPANS[group][-1] + 2):
                end = unpack_tail(self.keys[s, 192:208].astype(F32)).astype(BF16)
                pieces.append(jnp.concatenate([self.keys[s, 0:64], self.keys[s, 64:128], self.keys[s, 128:192], end], axis=1))
            rows_ = jnp.concatenate(pieces, axis=0)
            at = slice(128 * SPANS[group][0], 128 * SPANS[group][-1] + 128)
            key_rows[at] = rows_
            for t in range(4):
                self.weigh(group, at, rows_, t)

        def weigh(self, group, at, rows_, t):
            block = jnp.dot(rows_, query_t[:, tile(t)], preferred_element_type=F32)
            logits[at, tile(t)] = block
            top = jnp.max(jnp.max(fold(block), axis=0), axis=0, keepdims=True)
            if self.top[t] is not None:
                top = jnp.maximum(top, self.top[t])
            total = picked = jnp.zeros((8, 256), F32)
            for p in SPANS[group]:
                lines = slice(128 * p, 128 * p + 128)
                block = logits[lines, tile(t)]
                powers = jnp.exp(block - top)
                picked = picked + jnp.sum(fold(jnp.where(hits(self.r, p, t), block, 0.0)), axis=0)
                total = total + jnp.sum(fold(powers), axis=0)
                logits[lines, tile(t)] = powers
            if self.top[t] is not None:
                total = total + self.total[t] * jnp.exp(self.top[t] - top)
                picked = picked + self.picked[t]
            self.top[t], self.total[t], self.picked[t] = top, total, picked
            tops[group:group + 1, tile(t)] = top

        def flip(self, group):
            at = slice(128 * SPANS[group][0], 128 * SPANS[group][-1] + 128)
            keys_t[:, at] = key_rows[at].T

        def close(self):
            self.inverse = []
            for t in range(4):
                total = jnp.sum(self.total[t], axis=0, keepdims=True)
                picked = jnp.sum(self.picked[t], axis=0, keepdims=True)
                loss[self.r:self.r + 1, tile(t)] = self.top[t] + jnp.log(total) - picked
                self.inverse.append(1.0 / total)

        def spread(self, group, part):
            for t in range(4):
                factor = jnp.exp(tops[group:group + 1, tile(t)] - self.top[t]) * self.inverse[t]
                for p in SPANS[group]:
                    lines = slice(128 * p, 128 * p + 128)
                    share = logits[lines, tile(t)] * factor
                    resid[lines, tile(t)] = jnp.where(hits(self.r, p, t), share - 1.0, share).astype(BF16)
            at = slice(128 * SPANS[group][0], 128 * SPANS[group][-1] + 128)
            grad = jnp.dot(resid[at], query[...], preferred_element_type=F32)
            for p in range(2 * len(SPANS[group])):
                part[SPANS[group][0] + p // 2, p % 2] = pack(grad[SHARD * p:SHARD * p + SHARD]).astype(BF16)

    def learn(r, t):
        table, totals = (src, accum) if r == 0 else (new_src, new_accum)
        grad = jnp.dot(keys_t[0:D], resid[:, tile(t)], preferred_element_type=F32) * scale[r, :, tile(t)]
        sums = totals[:, tile(t)] + jnp.sum(grad * grad, axis=0, keepdims=True) * (1.0 / D)
        new_accum[:, tile(t)] = sums
        new_src[:, tile(t)] = table[:, tile(t)] - (LEARN_RATE * grad) / jnp.sqrt(sums)

    def wide_rows(x):
        return jnp.concatenate([x, jnp.zeros((SHARD, DP - D), F32)], axis=1)

    keys0[own] = pack(wide_rows(rows[...])).astype(BF16)
    query_t[D:DP] = jnp.zeros((DP - D, SRC), BF16)
    query[:, 384:DP] = jnp.zeros((SRC, DP - 384), BF16)
    greet(me)
    gather = first_gather = Gather(keys0, *sems[0:4], me)
    gather.start()
    for t in range(3):
        relate(0, t)
        ask(0, t)
    gather.relay(0)
    gather.relay(1)
    relate(0, 3)
    ask(0, 3)
    soft = Softmax(0, keys0)

    def rest_of_gather(gather, soft):
        gather.near(1, 0)
        gather.pair(3)
        soft.score(3)
        for col, dz in ((1, 1), (1, -1), (0, 1), (0, -1)):
            gather.near(col, dz)
        gather.far(0, 1)
        gather.far(1, 1)
        gather.pair(2)
        soft.score(2)
        gather.far(0, 2)
        gather.far(1, 2)
        gather.pair(1)
        soft.score(1)
        gather.pair(0)
        soft.score(0)
        soft.close()

    rest_of_gather(gather, soft)

    def rest_of_scatter(scatter, soft, part, r):
        soft.spread(0, part)
        scatter.pair(0)
        soft.spread(1, part)
        scatter.pair(1)
        scatter.far(1, 2)
        scatter.far(0, 2)
        scatter.far(1, 1)
        scatter.far(0, 1)
        soft.spread(2, part)
        scatter.pair(2)
        soft.spread(3, part)
        scatter.pair(3)
        for col, dz in ((1, 1), (1, -1), (0, 1), (0, -1)):
            scatter.near(col, dz)
        scatter.relay(1)
        scatter.near(1, 0)
        scatter.relay(0)
        for group in range(4):
            soft.flip(group)
        for t in range(4):
            learn(r, t)

    scatter = Scatter(part0, pair0, out0, in0, *sems[4:8], me)
    rest_of_scatter(scatter, soft, part0, 0)
    grad = scatter.finish()[:, 0:D]
    updated, total = adagrad_rows(rows[...], column_of(row_accum[...]), grad)
    key_row[...] = pack(wide_rows(updated)).astype(BF16)
    shift = remote(key_row, keys1.at[own], sems[16].at[0], sems[17].at[0], beyond)
    shift.start()
    moved[...] = wide_rows(updated)
    moved[:, 384:512] = jnp.where(lax.broadcasted_iota(I32, (SHARD, 128), 1) < 16, moved[:, 384:512], total)
    carry = remote(moved, landing, sems[16].at[1], sems[17].at[1], beyond)
    carry.start()
    relate(1, 0)
    relate(1, 1)
    shift.wait_recv()
    gather = Gather(keys1, *sems[8:12], me)
    gather.start()
    relate(1, 2)
    relate(1, 3)
    ask(1, 0)
    ask(1, 1)
    gather.relay(0)
    gather.relay(1)
    ask(1, 2)
    ask(1, 3)
    soft = Softmax(1, keys1)
    rest_of_gather(gather, soft)
    scatter = Scatter(part1, pair1, out1, in1, *sems[12:16], me)
    rest_of_scatter(scatter, soft, part1, 1)
    grad = scatter.finish()[:, 0:D]
    carry.wait_recv()
    updated, total = adagrad_rows(landing[:, 0:D], landing[:, D:D + 1], grad)
    new_rows[...] = updated
    new_row_accum[...] = row_of(total)
    carry.wait_send()
    first_gather.finish()
    gather.finish()
    shift.wait_send()


VM = pl.BlockSpec(memory_space=pltpu.VMEM)
DMA = pltpu.SemaphoreType.DMA


def hand_over(*arrays):
    def kernel(*refs):
        half = len(refs) // 2
        for source, target in zip(refs[:half], refs[half:]):
            target[...] = source[...]

    return pl.pallas_call(
        kernel,
        out_shape=[jax.ShapeDtypeStruct(a.shape, a.dtype) for a in arrays],
        in_specs=[VM] * len(arrays),
        out_specs=[VM] * len(arrays),
    )(*arrays)


def shards(src_rows, src_accum, dst_rows, dst_accum, relations, rel_ids, targets):
    twice = lambda shape, kind: [pltpu.VMEM(shape, kind)] * 2
    new_src, new_accum, new_rows, new_row_accum, loss = pl.pallas_call(
        train_kernel,
        out_shape=[
            jax.ShapeDtypeStruct(s, F32) for s in ((D, SRC), (1, SRC), (SHARD, D), (1, SHARD), (2, SRC))
        ],
        in_specs=[VM] * 7,
        out_specs=[VM] * 5,
        scratch_shapes=[
            pltpu.VMEM((2, D, SRC), F32), pltpu.VMEM((DP, SRC), BF16), pltpu.VMEM((SRC, DP), BF16),
            pltpu.VMEM((BUCKET, SRC), F32), pltpu.VMEM((BUCKET, SRC), BF16), pltpu.VMEM((DP, BUCKET), BF16),
            pltpu.VMEM((BUCKET, DP), BF16),
            *twice((32, SLOT, 128), BF16), *twice((CHIPS, 2, SLOT, 128), BF16), *twice((CHIPS, SLOT, 128), BF16),
            *twice((STEPS, SLOT, 128), BF16), *twice((STEPS, SLOT, 128), BF16),
            pltpu.VMEM((SLOT, 128), BF16), *twice((SHARD, DP), F32), pltpu.VMEM((8, SRC), F32),
            *([DMA((STEPS,)), DMA((STEPS,)), DMA((CHIPS,)), DMA((CHIPS,))] * 4), DMA((2,)), DMA((2,)),
        ],
        compiler_params=pltpu.CompilerParams(
            collective_id=0, has_side_effects=True, vmem_limit_bytes=62 * 1024 * 1024,
        ),
    )(src_rows.T, src_accum.reshape(1, SRC), dst_rows, dst_accum.reshape(1, SHARD), relations.T, rel_ids, targets)
    (new_src, new_accum, new_rows, new_row_accum, loss) = hand_over(new_src, new_accum, new_rows, new_row_accum, loss)
    return (new_src.T, new_accum.reshape(SRC), new_rows, new_row_accum.reshape(SHARD), loss)


def solution(mesh):
    both = ("grp", "wide")
    placed = (P(both, None), P(both), P(both, None), P(both), P(), P(None, both), P(None, both))
    return jax.shard_map(
        shards, mesh=mesh, in_specs=placed,
        out_specs=(P(both, None), P(both), P(both, None), P(both), P(None, both)),
        check_vma=False,
    )
```

```python
import jax
import jax.numpy as jnp
from jax import lax
from jax.experimental import pallas as pl
from jax.experimental.pallas import tpu as pltpu
from jax.sharding import PartitionSpec as P

MESH = pl.DeviceIdType.MESH
F32, BF16, I32 = jnp.float32, jnp.bfloat16, jnp.int32
LEARN_RATE = 0.1
D, DP = 400, 512
SRC, BUCKET, SHARD = 1024, 2048, 64
NZ, CHIPS = 8, 16
GROUPS = (
    ((1, 4), (0, 4)),
    ((1, 3), (1, -3), (0, 3), (0, -3)),
    ((0, 1), (0, -1), (1, 1), (1, -1)),
    ((1, 2), (1, -2), (0, 2), (0, -2), (1, 0), (0, 0)),
)
BLOCKS = sum(GROUPS, ())
SPOT = {(col, dz % NZ): p for p, (col, dz) in enumerate(BLOCKS)}
SPANS = tuple(range(sum(map(len, GROUPS[:n])), sum(map(len, GROUPS[:n + 1]))) for n in range(len(GROUPS)))
SLOT = 208
DIRECT = ((1, 2), (1, -2), (0, 2), (0, -2), (1, 0), (1, 1), (1, -1), (0, 1), (0, -1))
RELAYS = tuple((col, way, more) for col in (0, 1) for way in (1, -1) for more in (1, 2) if more == 1 or way == (1, -1)[col])
STEPS = len(DIRECT) + len(RELAYS) + 1
HOME = STEPS - 1


def spot(col, dz):
    return SPOT[(col, dz % NZ)]


def direct_at(col, dz):
    return DIRECT.index((col, dz))


def relay_at(col, way, more):
    return len(DIRECT) + RELAYS.index((col, way, more))


def pack(x):
    last = x[:, 384:512]
    tail = last[0:16]
    for q in range(1, 4):
        tail = tail + pltpu.roll(last[16 * q:16 * q + 16], 16 * q, 1)
    return jnp.concatenate([x[:, 0:128], x[:, 128:256], x[:, 256:384], tail], axis=0)


def unpack_tail(tail):
    keep = lax.broadcasted_iota(I32, (16, 128), 1) < 16
    parts = [tail] + [pltpu.roll(tail, 128 - 16 * q, 1) for q in range(1, 4)]
    return jnp.concatenate([jnp.where(keep, part, 0.0) for part in parts], axis=0)


def unpack(x):
    return jnp.concatenate([x[0:64], x[64:128], x[128:192], unpack_tail(x[192:208])], axis=1)


def place():
    g, w = lax.axis_index("grp"), lax.axis_index("wide")
    core = lax.rem(w, 2)
    z = lax.rem(lax.div(w, 2), NZ)
    y = lax.div(w, 2 * NZ)
    return g, y, z, core


def wide_of(y, z, core):
    return (y * NZ + z) * 2 + core


def wrap(z):
    return lax.rem(z + 2 * NZ, NZ)


def at(me, col, dz):
    g, y, z, core = me
    return wide_of(y if col == 0 else 1 - y, wrap(z + dz), core)


def greet(me):
    g, y, z, core = me
    n = lax.axis_size("grp")
    barrier = pltpu.get_barrier_semaphore()
    around = [at(me, col, dz) for col, dz in DIRECT]
    targets = [(g, w) for w in around + [wide_of(y, z, 1 - core)]]
    for other in (lax.rem(g + 1, n), lax.rem(g + n - 1, n)):
        targets.append((other, wide_of(y, z, core)))
    for target in targets:
        pl.semaphore_signal(barrier, inc=1, device_id=target, device_id_type=MESH)
    pl.semaphore_wait(barrier, len(targets))


def remote(src, dst, send, recv, target):
    return pltpu.make_async_remote_copy(
        src_ref=src, dst_ref=dst, send_sem=send, recv_sem=recv,
        device_id=target, device_id_type=MESH,
    )


class Gather:
    def __init__(self, keys, step_s, step_r, pair_s, pair_r, me):
        self.keys, self.sems, self.me, self.sent = keys, (step_s, step_r, pair_s, pair_r), me, []

    def copy(self, p, q, n, device, pair=False):
        core = self.me[3]
        send, recv = self.sems[2:] if pair else self.sems[:2]
        return remote(self.keys.at[2 * p + core], self.keys.at[2 * q + core], send.at[n], recv.at[n], device)

    def push(self, *args, **kwargs):
        copy = self.copy(*args, **kwargs)
        copy.start()
        self.sent.append(copy)

    def share(self, p):
        g, y, z, core = self.me
        self.push(p, p, p, (g, wide_of(y, z, 1 - core)), pair=True)

    def start(self):
        own = spot(0, 0)
        for col, dz in DIRECT:
            self.push(own, spot(col, -dz), direct_at(col, dz), (self.me[0], at(self.me, col, dz)))
        self.share(own)

    def wait(self, p, n):
        g, y, z, core = self.me
        self.copy(p, p, n, (g, wide_of(y, z, 1 - core))).wait_recv()

    def relay(self, col):
        for way in (1, -1):
            p = spot(col, -2 * way)
            self.wait(p, direct_at(col, 2 * way))
            for more in (2, 1):
                if (col, way, more) in RELAYS:
                    self.push(p, spot(col, -way * (2 + more)), relay_at(col, way, more), (self.me[0], at(self.me, 0, way * more)))
            self.share(p)

    def near(self, col, dz):
        p = spot(col, -dz)
        self.wait(p, direct_at(col, dz))
        self.share(p)

    def far(self, col, more):
        for way in (1, -1):
            if (col, way, more) in RELAYS:
                p = spot(col, -way * (2 + more))
                self.wait(p, relay_at(col, way, more))
                self.share(p)

    def pair(self, group):
        g, y, z, core = self.me
        for p in SPANS[group]:
            slot = self.keys.at[2 * p + 1 - core]
            remote(slot, slot, self.sems[2].at[p], self.sems[3].at[p], (g, wide_of(y, z, 1 - core))).wait_recv()

    def finish(self):
        for copy in self.sent:
            copy.wait_send()


class Scatter:
    def __init__(self, part, from_pair, out_sum, inbox, step_s, step_r, pair_s, pair_r, me):
        self.part, self.from_pair, self.out_sum, self.inbox = part, from_pair, out_sum, inbox
        self.sems, self.me, self.sent = (step_s, step_r, pair_s, pair_r), me, []

    def swap(self, p):
        g, y, z, core = self.me
        return remote(self.part.at[p, 1 - core], self.from_pair.at[p], self.sems[2].at[p], self.sems[3].at[p],
                      (g, wide_of(y, z, 1 - core)))

    def pair(self, group):
        for p in SPANS[group]:
            copy = self.swap(p)
            copy.start()
            self.sent.append(copy)

    def mine(self, col, dz):
        p = spot(col, dz)
        self.swap(p).wait_recv()
        return self.part[p, self.me[3]].astype(F32) + self.from_pair[p].astype(F32)

    def step(self, n, w):
        return remote(self.out_sum.at[n], self.inbox.at[n], self.sems[0].at[n], self.sems[1].at[n], (self.me[0], w))

    def arrived(self, n):
        self.step(n, at(self.me, 0, 1)).wait_recv()
        return self.inbox[n].astype(F32)

    def send(self, n, total, w):
        self.out_sum[n] = total.astype(BF16)
        copy = self.step(n, w)
        copy.start()
        self.sent.append(copy)

    def far(self, col, more):
        for way in (1, -1):
            if (col, way, more) in RELAYS:
                self.send(relay_at(col, way, more), self.mine(col, way * (2 + more)), at(self.me, 0, way * more))

    def relay(self, col):
        for way in (1, -1):
            total = self.mine(col, 2 * way)
            for more in (1, 2):
                if (col, way, more) in RELAYS:
                    total = total + self.arrived(relay_at(col, way, more))
            self.send(direct_at(col, 2 * way), total, at(self.me, col, 2 * way))

    def near(self, col, dz):
        self.send(direct_at(col, dz), self.mine(col, dz), at(self.me, col, dz))

    def finish(self):
        total = self.mine(0, 0)
        for col, dz in ((0, 1), (0, -1), (1, 0), (1, 1), (1, -1), (0, 2), (0, -2), (1, 2), (1, -2)):
            total = total + self.arrived(direct_at(col, dz))
        for copy in self.sent:
            copy.wait_send()
        return unpack(total)


def column_of(row):
    n = row.shape[1]
    same = lax.broadcasted_iota(I32, (n, n), 0) == lax.broadcasted_iota(I32, (n, n), 1)
    return jnp.sum(jnp.where(same, row, 0.0), axis=1, keepdims=True)


def row_of(column):
    n = column.shape[0]
    same = lax.broadcasted_iota(I32, (n, n), 0) == lax.broadcasted_iota(I32, (n, n), 1)
    return jnp.sum(jnp.where(same, column, 0.0), axis=0, keepdims=True)


def adagrad_rows(rows, accum, grad):
    accum = accum + jnp.sum(grad * grad, axis=1, keepdims=True) * (1.0 / D)
    return rows - (LEARN_RATE * grad) / jnp.sqrt(accum), accum


def train_kernel(src, accum, rows, row_accum, rels, ids, labels,
                 new_src, new_accum, new_rows, new_row_accum, loss,
                 scale, query_t, query, logits, resid, keys_t, key_rows,
                 keys0, keys1, part0, part1, pair0, pair1, out0, out1, in0, in1, key_row, moved, landing, tops,
                 *sems):
    me = g, y, z, core = place()
    here = wide_of(y, z, core)
    beyond = (lax.rem(g + 1, lax.axis_size("grp")), here)
    own = 2 * spot(0, 0) + core

    def tile(t):
        return slice(256 * t, 256 * t + 256)

    def relate(r, t):
        hot = (lax.broadcasted_iota(I32, (SRC, 256), 0) == ids[r:r + 1, tile(t)]).astype(BF16)
        total = jnp.zeros((D, 256), F32)
        rest = rels[...]
        for _ in range(3):
            piece = rest.astype(BF16)
            rest = rest - piece.astype(F32)
            total = total + jnp.dot(piece, hot, preferred_element_type=F32)
        scale[r, :, tile(t)] = total

    def ask(r, t):
        table = src if r == 0 else new_src
        quarter = (table[:, tile(t)] * scale[r, :, tile(t)]).astype(BF16)
        query_t[0:D, tile(t)] = quarter
        query[tile(t), 0:D] = quarter.T

    def hits(r, p, t):
        col, dz = BLOCKS[p]
        chip = (y if col == 0 else 1 - y) * NZ + wrap(z + dz)
        return lax.broadcasted_iota(I32, (128, 256), 0) == labels[r:r + 1, tile(t)] - 128 * chip

    def fold(x):
        return x.reshape(-1, 8, x.shape[1])

    class Softmax:
        def __init__(self, r, keys):
            self.r, self.keys = r, keys
            self.top, self.total, self.picked = [None] * 4, [None] * 4, [None] * 4

        def score(self, group):
            pieces = []
            for s in range(2 * SPANS[group][0], 2 * SPANS[group][-1] + 2):
                end = unpack_tail(self.keys[s, 192:208].astype(F32)).astype(BF16)
                pieces.append(jnp.concatenate([self.keys[s, 0:64], self.keys[s, 64:128], self.keys[s, 128:192], end], axis=1))
            rows_ = jnp.concatenate(pieces, axis=0)
            at = slice(128 * SPANS[group][0], 128 * SPANS[group][-1] + 128)
            key_rows[at] = rows_
            for t in range(4):
                self.weigh(group, at, rows_, t)

        def weigh(self, group, at, rows_, t):
            block = jnp.dot(rows_, query_t[:, tile(t)], preferred_element_type=F32)
            logits[at, tile(t)] = block
            top = jnp.max(jnp.max(fold(block), axis=0), axis=0, keepdims=True)
            if self.top[t] is not None:
                top = jnp.maximum(top, self.top[t])
            total = picked = jnp.zeros((8, 256), F32)
            for p in SPANS[group]:
                lines = slice(128 * p, 128 * p + 128)
                block = logits[lines, tile(t)]
                powers = jnp.exp(block - top)
                picked = picked + jnp.sum(fold(jnp.where(hits(self.r, p, t), block, 0.0)), axis=0)
                total = total + jnp.sum(fold(powers), axis=0)
                logits[lines, tile(t)] = powers
            if self.top[t] is not None:
                total = total + self.total[t] * jnp.exp(self.top[t] - top)
                picked = picked + self.picked[t]
            self.top[t], self.total[t], self.picked[t] = top, total, picked
            tops[group:group + 1, tile(t)] = top

        def flip(self, group):
            at = slice(128 * SPANS[group][0], 128 * SPANS[group][-1] + 128)
            keys_t[:, at] = key_rows[at].T

        def close(self):
            self.inverse = []
            for t in range(4):
                total = jnp.sum(self.total[t], axis=0, keepdims=True)
                picked = jnp.sum(self.picked[t], axis=0, keepdims=True)
                loss[self.r:self.r + 1, tile(t)] = self.top[t] + jnp.log(total) - picked
                self.inverse.append(1.0 / total)

        def spread(self, group, part):
            for t in range(4):
                factor = jnp.exp(tops[group:group + 1, tile(t)] - self.top[t]) * self.inverse[t]
                for p in SPANS[group]:
                    lines = slice(128 * p, 128 * p + 128)
                    share = logits[lines, tile(t)] * factor
                    resid[lines, tile(t)] = jnp.where(hits(self.r, p, t), share - 1.0, share).astype(BF16)
            at = slice(128 * SPANS[group][0], 128 * SPANS[group][-1] + 128)
            grad = jnp.dot(resid[at], query[...], preferred_element_type=F32)
            for p in range(2 * len(SPANS[group])):
                part[SPANS[group][0] + p // 2, p % 2] = pack(grad[SHARD * p:SHARD * p + SHARD]).astype(BF16)

    def learn(r, t):
        table, totals = (src, accum) if r == 0 else (new_src, new_accum)
        grad = jnp.dot(keys_t[0:D], resid[:, tile(t)], preferred_element_type=F32) * scale[r, :, tile(t)]
        sums = totals[:, tile(t)] + jnp.sum(grad * grad, axis=0, keepdims=True) * (1.0 / D)
        new_accum[:, tile(t)] = sums
        new_src[:, tile(t)] = table[:, tile(t)] - (LEARN_RATE * grad) / jnp.sqrt(sums)

    def wide_rows(x):
        return jnp.concatenate([x, jnp.zeros((SHARD, DP - D), F32)], axis=1)

    keys0[own] = pack(wide_rows(rows[...])).astype(BF16)
    query_t[D:DP] = jnp.zeros((DP - D, SRC), BF16)
    query[:, 384:DP] = jnp.zeros((SRC, DP - 384), BF16)
    greet(me)
    gather = first_gather = Gather(keys0, *sems[0:4], me)
    gather.start()
    for t in range(3):
        relate(0, t)
        ask(0, t)
    gather.relay(0)
    gather.relay(1)
    relate(0, 3)
    ask(0, 3)
    soft = Softmax(0, keys0)

    def rest_of_gather(gather, soft):
        gather.near(1, 0)
        gather.pair(3)
        soft.score(3)
        for col, dz in ((1, 1), (1, -1), (0, 1), (0, -1)):
            gather.near(col, dz)
        gather.far(0, 1)
        gather.far(1, 1)
        gather.pair(2)
        soft.score(2)
        gather.far(0, 2)
        gather.far(1, 2)
        gather.pair(1)
        soft.score(1)
        gather.pair(0)
        soft.score(0)
        soft.close()

    rest_of_gather(gather, soft)

    def rest_of_scatter(scatter, soft, part, r):
        soft.spread(0, part)
        scatter.pair(0)
        soft.spread(1, part)
        scatter.pair(1)
        scatter.far(1, 2)
        scatter.far(0, 2)
        scatter.far(1, 1)
        scatter.far(0, 1)
        soft.spread(2, part)
        scatter.pair(2)
        soft.spread(3, part)
        scatter.pair(3)
        scatter.near(1, 1)
        scatter.near(1, -1)
        scatter.relay(1)
        scatter.relay(0)
        scatter.near(0, 1)
        scatter.near(0, -1)
        scatter.near(1, 0)
        for group in range(4):
            soft.flip(group)
        for t in range(4):
            learn(r, t)

    scatter = Scatter(part0, pair0, out0, in0, *sems[4:8], me)
    rest_of_scatter(scatter, soft, part0, 0)
    grad = scatter.finish()[:, 0:D]
    updated, total = adagrad_rows(rows[...], column_of(row_accum[...]), grad)
    key_row[...] = pack(wide_rows(updated)).astype(BF16)
    shift = remote(key_row, keys1.at[own], sems[16].at[0], sems[17].at[0], beyond)
    shift.start()
    moved[...] = wide_rows(updated)
    moved[:, 384:512] = jnp.where(lax.broadcasted_iota(I32, (SHARD, 128), 1) < 16, moved[:, 384:512], total)
    carry = remote(moved, landing, sems[16].at[1], sems[17].at[1], beyond)
    carry.start()
    relate(1, 0)
    relate(1, 1)
    shift.wait_recv()
    gather = Gather(keys1, *sems[8:12], me)
    gather.start()
    relate(1, 2)
    relate(1, 3)
    ask(1, 0)
    ask(1, 1)
    gather.relay(0)
    gather.relay(1)
    ask(1, 2)
    ask(1, 3)
    soft = Softmax(1, keys1)
    rest_of_gather(gather, soft)
    scatter = Scatter(part1, pair1, out1, in1, *sems[12:16], me)
    rest_of_scatter(scatter, soft, part1, 1)
    grad = scatter.finish()[:, 0:D]
    carry.wait_recv()
    updated, total = adagrad_rows(landing[:, 0:D], landing[:, D:D + 1], grad)
    new_rows[...] = updated
    new_row_accum[...] = row_of(total)
    carry.wait_send()
    first_gather.finish()
    gather.finish()
    shift.wait_send()


VM = pl.BlockSpec(memory_space=pltpu.VMEM)
DMA = pltpu.SemaphoreType.DMA


def hand_over(*arrays):
    def kernel(*refs):
        half = len(refs) // 2
        for source, target in zip(refs[:half], refs[half:]):
            target[...] = source[...]

    return pl.pallas_call(
        kernel,
        out_shape=[jax.ShapeDtypeStruct(a.shape, a.dtype) for a in arrays],
        in_specs=[VM] * len(arrays),
        out_specs=[VM] * len(arrays),
    )(*arrays)


def shards(src_rows, src_accum, dst_rows, dst_accum, relations, rel_ids, targets):
    twice = lambda shape, kind: [pltpu.VMEM(shape, kind)] * 2
    new_src, new_accum, new_rows, new_row_accum, loss = pl.pallas_call(
        train_kernel,
        out_shape=[
            jax.ShapeDtypeStruct(s, F32) for s in ((D, SRC), (1, SRC), (SHARD, D), (1, SHARD), (2, SRC))
        ],
        in_specs=[VM] * 7,
        out_specs=[VM] * 5,
        scratch_shapes=[
            pltpu.VMEM((2, D, SRC), F32), pltpu.VMEM((DP, SRC), BF16), pltpu.VMEM((SRC, DP), BF16),
            pltpu.VMEM((BUCKET, SRC), F32), pltpu.VMEM((BUCKET, SRC), BF16), pltpu.VMEM((DP, BUCKET), BF16),
            pltpu.VMEM((BUCKET, DP), BF16),
            *twice((32, SLOT, 128), BF16), *twice((CHIPS, 2, SLOT, 128), BF16), *twice((CHIPS, SLOT, 128), BF16),
            *twice((STEPS, SLOT, 128), BF16), *twice((STEPS, SLOT, 128), BF16),
            pltpu.VMEM((SLOT, 128), BF16), *twice((SHARD, DP), F32), pltpu.VMEM((8, SRC), F32),
            *([DMA((STEPS,)), DMA((STEPS,)), DMA((CHIPS,)), DMA((CHIPS,))] * 4), DMA((2,)), DMA((2,)),
        ],
        compiler_params=pltpu.CompilerParams(
            collective_id=0, has_side_effects=True, vmem_limit_bytes=62 * 1024 * 1024,
        ),
    )(src_rows.T, src_accum.reshape(1, SRC), dst_rows, dst_accum.reshape(1, SHARD), relations.T, rel_ids, targets)
    (new_src, new_accum, new_rows, new_row_accum, loss) = hand_over(new_src, new_accum, new_rows, new_row_accum, loss)
    return (new_src.T, new_accum.reshape(SRC), new_rows, new_row_accum.reshape(SHARD), loss)


def solution(mesh):
    both = ("grp", "wide")
    placed = (P(both, None), P(both), P(both, None), P(both), P(), P(None, both), P(None, both))
    return jax.shard_map(
        shards, mesh=mesh, in_specs=placed,
        out_specs=(P(both, None), P(both), P(both, None), P(both), P(None, both)),
        check_vma=False,
    )
```

```python
import jax
import jax.numpy as jnp
from jax import lax
from jax.experimental import pallas as pl
from jax.experimental.pallas import tpu as pltpu
from jax.sharding import PartitionSpec as P

MESH = pl.DeviceIdType.MESH
F32, BF16, I32 = jnp.float32, jnp.bfloat16, jnp.int32
LEARN_RATE = 0.1
D, DP = 400, 512
SRC, BUCKET, SHARD = 1024, 2048, 64
NZ, CHIPS = 8, 16
GROUPS = (
    ((1, 4), (0, 4)),
    ((1, 3), (1, -3), (0, 3), (0, -3)),
    ((0, 1), (0, -1), (1, 1), (1, -1)),
    ((1, 2), (1, -2), (0, 2), (0, -2), (1, 0), (0, 0)),
)
BLOCKS = sum(GROUPS, ())
SPOT = {(col, dz % NZ): p for p, (col, dz) in enumerate(BLOCKS)}
SPANS = tuple(range(sum(map(len, GROUPS[:n])), sum(map(len, GROUPS[:n + 1]))) for n in range(len(GROUPS)))
SLOT = 208
DIRECT = ((1, 2), (1, -2), (0, 2), (0, -2), (1, 0), (1, 1), (1, -1), (0, 1), (0, -1))
RELAYS = tuple((col, way, more) for col in (0, 1) for way in (1, -1) for more in (1, 2) if more == 1 or way == (1, -1)[col])
STEPS = len(DIRECT) + len(RELAYS) + 1
HOME = STEPS - 1


def spot(col, dz):
    return SPOT[(col, dz % NZ)]


def direct_at(col, dz):
    return DIRECT.index((col, dz))


def relay_at(col, way, more):
    return len(DIRECT) + RELAYS.index((col, way, more))


def pack(x):
    last = x[:, 384:512]
    tail = last[0:16]
    for q in range(1, 4):
        tail = tail + pltpu.roll(last[16 * q:16 * q + 16], 16 * q, 1)
    return jnp.concatenate([x[:, 0:128], x[:, 128:256], x[:, 256:384], tail], axis=0)


def unpack_tail(tail):
    keep = lax.broadcasted_iota(I32, (16, 128), 1) < 16
    parts = [tail] + [pltpu.roll(tail, 128 - 16 * q, 1) for q in range(1, 4)]
    return jnp.concatenate([jnp.where(keep, part, 0.0) for part in parts], axis=0)


def unpack(x):
    return jnp.concatenate([x[0:64], x[64:128], x[128:192], unpack_tail(x[192:208])], axis=1)


def place():
    g, w = lax.axis_index("grp"), lax.axis_index("wide")
    core = lax.rem(w, 2)
    z = lax.rem(lax.div(w, 2), NZ)
    y = lax.div(w, 2 * NZ)
    return g, y, z, core


def wide_of(y, z, core):
    return (y * NZ + z) * 2 + core


def wrap(z):
    return lax.rem(z + 2 * NZ, NZ)


def at(me, col, dz):
    g, y, z, core = me
    return wide_of(y if col == 0 else 1 - y, wrap(z + dz), core)


def greet(me):
    g, y, z, core = me
    n = lax.axis_size("grp")
    barrier = pltpu.get_barrier_semaphore()
    around = [at(me, col, dz) for col, dz in DIRECT]
    targets = [(g, w) for w in around + [wide_of(y, z, 1 - core)]]
    for other in (lax.rem(g + 1, n), lax.rem(g + n - 1, n)):
        targets.append((other, wide_of(y, z, core)))
    for target in targets:
        pl.semaphore_signal(barrier, inc=1, device_id=target, device_id_type=MESH)
    pl.semaphore_wait(barrier, len(targets))


def remote(src, dst, send, recv, target):
    return pltpu.make_async_remote_copy(
        src_ref=src, dst_ref=dst, send_sem=send, recv_sem=recv,
        device_id=target, device_id_type=MESH,
    )


class Gather:
    def __init__(self, keys, step_s, step_r, pair_s, pair_r, me):
        self.keys, self.sems, self.me, self.sent = keys, (step_s, step_r, pair_s, pair_r), me, []

    def copy(self, p, q, n, device, pair=False):
        core = self.me[3]
        send, recv = self.sems[2:] if pair else self.sems[:2]
        return remote(self.keys.at[2 * p + core], self.keys.at[2 * q + core], send.at[n], recv.at[n], device)

    def push(self, *args, **kwargs):
        copy = self.copy(*args, **kwargs)
        copy.start()
        self.sent.append(copy)

    def share(self, p):
        g, y, z, core = self.me
        self.push(p, p, p, (g, wide_of(y, z, 1 - core)), pair=True)

    def start(self):
        own = spot(0, 0)
        for col, dz in DIRECT:
            self.push(own, spot(col, -dz), direct_at(col, dz), (self.me[0], at(self.me, col, dz)))
        self.share(own)

    def wait(self, p, n):
        g, y, z, core = self.me
        self.copy(p, p, n, (g, wide_of(y, z, 1 - core))).wait_recv()

    def relay(self, col):
        for way in (1, -1):
            p = spot(col, -2 * way)
            self.wait(p, direct_at(col, 2 * way))
            for more in (2, 1):
                if (col, way, more) in RELAYS:
                    self.push(p, spot(col, -way * (2 + more)), relay_at(col, way, more), (self.me[0], at(self.me, 0, way * more)))
            self.share(p)

    def near(self, col, dz):
        p = spot(col, -dz)
        self.wait(p, direct_at(col, dz))
        self.share(p)

    def far(self, col, more):
        for way in (1, -1):
            if (col, way, more) in RELAYS:
                p = spot(col, -way * (2 + more))
                self.wait(p, relay_at(col, way, more))
                self.share(p)

    def pair(self, group):
        g, y, z, core = self.me
        for p in SPANS[group]:
            slot = self.keys.at[2 * p + 1 - core]
            remote(slot, slot, self.sems[2].at[p], self.sems[3].at[p], (g, wide_of(y, z, 1 - core))).wait_recv()

    def finish(self):
        for copy in self.sent:
            copy.wait_send()


class Scatter:
    def __init__(self, part, from_pair, out_sum, inbox, step_s, step_r, pair_s, pair_r, me):
        self.part, self.from_pair, self.out_sum, self.inbox = part, from_pair, out_sum, inbox
        self.sems, self.me, self.sent = (step_s, step_r, pair_s, pair_r), me, []

    def swap(self, p):
        g, y, z, core = self.me
        return remote(self.part.at[p, 1 - core], self.from_pair.at[p], self.sems[2].at[p], self.sems[3].at[p],
                      (g, wide_of(y, z, 1 - core)))

    def pair(self, group):
        for p in SPANS[group]:
            copy = self.swap(p)
            copy.start()
            self.sent.append(copy)

    def mine(self, col, dz):
        p = spot(col, dz)
        self.swap(p).wait_recv()
        return self.part[p, self.me[3]].astype(F32) + self.from_pair[p].astype(F32)

    def step(self, n, w):
        return remote(self.out_sum.at[n], self.inbox.at[n], self.sems[0].at[n], self.sems[1].at[n], (self.me[0], w))

    def arrived(self, n):
        self.step(n, at(self.me, 0, 1)).wait_recv()
        return self.inbox[n].astype(F32)

    def send(self, n, total, w):
        self.out_sum[n] = total.astype(BF16)
        copy = self.step(n, w)
        copy.start()
        self.sent.append(copy)

    def far(self, col, more):
        for way in (1, -1):
            if (col, way, more) in RELAYS:
                self.send(relay_at(col, way, more), self.mine(col, way * (2 + more)), at(self.me, 0, way * more))

    def relay(self, col):
        for way in (1, -1):
            total = self.mine(col, 2 * way)
            for more in (1, 2):
                if (col, way, more) in RELAYS:
                    total = total + self.arrived(relay_at(col, way, more))
            self.send(direct_at(col, 2 * way), total, at(self.me, col, 2 * way))

    def near(self, col, dz):
        self.send(direct_at(col, dz), self.mine(col, dz), at(self.me, col, dz))

    def finish(self):
        total = self.mine(0, 0)
        for col, dz in ((0, 1), (0, -1), (1, 0), (1, 1), (1, -1), (0, 2), (0, -2), (1, 2), (1, -2)):
            total = total + self.arrived(direct_at(col, dz))
        for copy in self.sent:
            copy.wait_send()
        return unpack(total)


def column_of(row):
    n = row.shape[1]
    same = lax.broadcasted_iota(I32, (n, n), 0) == lax.broadcasted_iota(I32, (n, n), 1)
    return jnp.sum(jnp.where(same, row, 0.0), axis=1, keepdims=True)


def row_of(column):
    n = column.shape[0]
    same = lax.broadcasted_iota(I32, (n, n), 0) == lax.broadcasted_iota(I32, (n, n), 1)
    return jnp.sum(jnp.where(same, column, 0.0), axis=0, keepdims=True)


def adagrad_rows(rows, accum, grad):
    accum = accum + jnp.sum(grad * grad, axis=1, keepdims=True) * (1.0 / D)
    return rows - (LEARN_RATE * grad) / jnp.sqrt(accum), accum


def train_kernel(src, accum, rows, row_accum, rels, ids, labels,
                 new_src, new_accum, new_rows, new_row_accum, loss,
                 scale, query_t, query, logits, resid, keys_t, key_rows,
                 keys0, keys1, part0, part1, pair0, pair1, out0, out1, in0, in1, key_row, moved, landing, tops,
                 *sems):
    me = g, y, z, core = place()
    here = wide_of(y, z, core)
    beyond = (lax.rem(g + 1, lax.axis_size("grp")), here)
    own = 2 * spot(0, 0) + core

    def tile(t):
        return slice(256 * t, 256 * t + 256)

    def relate(r, t):
        hot = (lax.broadcasted_iota(I32, (SRC, 256), 0) == ids[r:r + 1, tile(t)]).astype(BF16)
        total = jnp.zeros((D, 256), F32)
        rest = rels[...]
        for _ in range(3):
            piece = rest.astype(BF16)
            rest = rest - piece.astype(F32)
            total = total + jnp.dot(piece, hot, preferred_element_type=F32)
        scale[r, :, tile(t)] = total

    def ask(r, t):
        table = src if r == 0 else new_src
        quarter = (table[:, tile(t)] * scale[r, :, tile(t)]).astype(BF16)
        query_t[0:D, tile(t)] = quarter
        query[tile(t), 0:D] = quarter.T

    def hits(r, p, t):
        col, dz = BLOCKS[p]
        chip = (y if col == 0 else 1 - y) * NZ + wrap(z + dz)
        return lax.broadcasted_iota(I32, (128, 256), 0) == labels[r:r + 1, tile(t)] - 128 * chip

    def fold(x):
        return x.reshape(-1, 8, x.shape[1])

    class Softmax:
        def __init__(self, r, keys):
            self.r, self.keys = r, keys
            self.top, self.total, self.picked = [None] * 4, [None] * 4, [None] * 4

        def score(self, group):
            pieces = []
            for s in range(2 * SPANS[group][0], 2 * SPANS[group][-1] + 2):
                end = unpack_tail(self.keys[s, 192:208].astype(F32)).astype(BF16)
                pieces.append(jnp.concatenate([self.keys[s, 0:64], self.keys[s, 64:128], self.keys[s, 128:192], end], axis=1))
            rows_ = jnp.concatenate(pieces, axis=0)
            at = slice(128 * SPANS[group][0], 128 * SPANS[group][-1] + 128)
            key_rows[at] = rows_
            for t in range(4):
                self.weigh(group, at, rows_, t)

        def weigh(self, group, at, rows_, t):
            block = jnp.dot(rows_, query_t[:, tile(t)], preferred_element_type=F32)
            logits[at, tile(t)] = block
            top = jnp.max(jnp.max(fold(block), axis=0), axis=0, keepdims=True)
            if self.top[t] is not None:
                top = jnp.maximum(top, self.top[t])
            total = picked = jnp.zeros((8, 256), F32)
            for p in SPANS[group]:
                lines = slice(128 * p, 128 * p + 128)
                block = logits[lines, tile(t)]
                powers = jnp.exp(block - top)
                picked = picked + jnp.sum(fold(jnp.where(hits(self.r, p, t), block, 0.0)), axis=0)
                total = total + jnp.sum(fold(powers), axis=0)
                logits[lines, tile(t)] = powers
            if self.top[t] is not None:
                total = total + self.total[t] * jnp.exp(self.top[t] - top)
                picked = picked + self.picked[t]
            self.top[t], self.total[t], self.picked[t] = top, total, picked
            tops[group:group + 1, tile(t)] = top

        def flip(self, group):
            at = slice(128 * SPANS[group][0], 128 * SPANS[group][-1] + 128)
            keys_t[:, at] = key_rows[at].T

        def close(self):
            self.inverse = []
            for t in range(4):
                total = jnp.sum(self.total[t], axis=0, keepdims=True)
                picked = jnp.sum(self.picked[t], axis=0, keepdims=True)
                loss[self.r:self.r + 1, tile(t)] = self.top[t] + jnp.log(total) - picked
                self.inverse.append(1.0 / total)

        def spread(self, group, part):
            for t in range(4):
                factor = jnp.exp(tops[group:group + 1, tile(t)] - self.top[t]) * self.inverse[t]
                for p in SPANS[group]:
                    lines = slice(128 * p, 128 * p + 128)
                    share = logits[lines, tile(t)] * factor
                    resid[lines, tile(t)] = jnp.where(hits(self.r, p, t), share - 1.0, share).astype(BF16)
            at = slice(128 * SPANS[group][0], 128 * SPANS[group][-1] + 128)
            grad = jnp.dot(resid[at], query[...], preferred_element_type=F32)
            for p in range(2 * len(SPANS[group])):
                part[SPANS[group][0] + p // 2, p % 2] = pack(grad[SHARD * p:SHARD * p + SHARD]).astype(BF16)

    def learn(r, t):
        table, totals = (src, accum) if r == 0 else (new_src, new_accum)
        grad = jnp.dot(keys_t[0:D], resid[:, tile(t)], preferred_element_type=F32) * scale[r, :, tile(t)]
        sums = totals[:, tile(t)] + jnp.sum(grad * grad, axis=0, keepdims=True) * (1.0 / D)
        new_accum[:, tile(t)] = sums
        new_src[:, tile(t)] = table[:, tile(t)] - (LEARN_RATE * grad) / jnp.sqrt(sums)

    def wide_rows(x):
        return jnp.concatenate([x, jnp.zeros((SHARD, DP - D), F32)], axis=1)

    keys0[own] = pack(wide_rows(rows[...])).astype(BF16)
    query_t[D:DP] = jnp.zeros((DP - D, SRC), BF16)
    query[:, 384:DP] = jnp.zeros((SRC, DP - 384), BF16)
    greet(me)
    gather = first_gather = Gather(keys0, *sems[0:4], me)
    gather.start()
    for t in range(3):
        relate(0, t)
        ask(0, t)
    gather.relay(0)
    gather.relay(1)
    relate(0, 3)
    ask(0, 3)
    soft = Softmax(0, keys0)

    def rest_of_gather(gather, soft):
        gather.near(1, 0)
        gather.pair(3)
        soft.score(3)
        for col, dz in ((1, 1), (1, -1), (0, 1), (0, -1)):
            gather.near(col, dz)
        gather.far(0, 1)
        gather.far(1, 1)
        gather.pair(2)
        soft.score(2)
        gather.far(0, 2)
        gather.far(1, 2)
        gather.pair(1)
        soft.score(1)
        gather.pair(0)
        soft.score(0)
        soft.close()

    rest_of_gather(gather, soft)

    def rest_of_scatter(scatter, soft, part, r):
        soft.spread(0, part)
        scatter.pair(0)
        soft.spread(1, part)
        scatter.pair(1)
        scatter.far(1, 2)
        scatter.far(0, 2)
        scatter.far(1, 1)
        scatter.far(0, 1)
        soft.spread(2, part)
        scatter.pair(2)
        soft.spread(3, part)
        scatter.pair(3)
        scatter.near(1, 1)
        scatter.near(1, -1)
        scatter.relay(1)
        scatter.relay(0)
        scatter.near(0, 1)
        scatter.near(0, -1)
        scatter.near(1, 0)
        for group in range(4):
            soft.flip(group)
        for t in range(4):
            learn(r, t)

    scatter = Scatter(part0, pair0, out0, in0, *sems[4:8], me)
    rest_of_scatter(scatter, soft, part0, 0)
    grad = scatter.finish()[:, 0:D]
    updated, total = adagrad_rows(rows[...], column_of(row_accum[...]), grad)
    key_row[...] = pack(wide_rows(updated)).astype(BF16)
    shift = remote(key_row, keys1.at[own], sems[16].at[0], sems[17].at[0], beyond)
    shift.start()
    moved[...] = wide_rows(updated)
    moved[:, 384:512] = jnp.where(lax.broadcasted_iota(I32, (SHARD, 128), 1) < 16, moved[:, 384:512], total)
    carry = remote(moved, landing, sems[16].at[1], sems[17].at[1], beyond)
    carry.start()
    relate(1, 0)
    relate(1, 1)
    shift.wait_recv()
    gather = Gather(keys1, *sems[8:12], me)
    gather.start()
    relate(1, 2)
    relate(1, 3)
    ask(1, 0)
    ask(1, 1)
    gather.relay(0)
    gather.relay(1)
    ask(1, 2)
    ask(1, 3)
    soft = Softmax(1, keys1)
    rest_of_gather(gather, soft)
    scatter = Scatter(part1, pair1, out1, in1, *sems[12:16], me)
    rest_of_scatter(scatter, soft, part1, 1)
    grad = scatter.finish()[:, 0:D]
    carry.wait_recv()
    updated, total = adagrad_rows(landing[:, 0:D], landing[:, D:D + 1], grad)
    new_rows[...] = updated
    new_row_accum[...] = row_of(total)
    carry.wait_send()
    first_gather.finish()
    gather.finish()
    shift.wait_send()


VM = pl.BlockSpec(memory_space=pltpu.VMEM)
DMA = pltpu.SemaphoreType.DMA


def hand_over(*arrays):
    def kernel(*refs):
        half = len(refs) // 2
        for source, target in zip(refs[:half], refs[half:]):
            target[...] = source[...]

    blocks = [pl.BlockSpec((D, SRC // 4), lambda t: (0, t))]
    blocks += [pl.BlockSpec(a.shape, lambda t: (0, 0)) for a in arrays[1:]]
    return pl.pallas_call(
        kernel,
        out_shape=[jax.ShapeDtypeStruct(a.shape, a.dtype) for a in arrays],
        grid=(4,),
        in_specs=blocks,
        out_specs=blocks,
    )(*arrays)


def shards(src_rows, src_accum, dst_rows, dst_accum, relations, rel_ids, targets):
    twice = lambda shape, kind: [pltpu.VMEM(shape, kind)] * 2
    new_src, new_accum, new_rows, new_row_accum, loss = pl.pallas_call(
        train_kernel,
        out_shape=[
            jax.ShapeDtypeStruct(s, F32) for s in ((D, SRC), (1, SRC), (SHARD, D), (1, SHARD), (2, SRC))
        ],
        in_specs=[VM] * 7,
        out_specs=[VM] * 5,
        scratch_shapes=[
            pltpu.VMEM((2, D, SRC), F32), pltpu.VMEM((DP, SRC), BF16), pltpu.VMEM((SRC, DP), BF16),
            pltpu.VMEM((BUCKET, SRC), F32), pltpu.VMEM((BUCKET, SRC), BF16), pltpu.VMEM((DP, BUCKET), BF16),
            pltpu.VMEM((BUCKET, DP), BF16),
            *twice((32, SLOT, 128), BF16), *twice((CHIPS, 2, SLOT, 128), BF16), *twice((CHIPS, SLOT, 128), BF16),
            *twice((STEPS, SLOT, 128), BF16), *twice((STEPS, SLOT, 128), BF16),
            pltpu.VMEM((SLOT, 128), BF16), *twice((SHARD, DP), F32), pltpu.VMEM((8, SRC), F32),
            *([DMA((STEPS,)), DMA((STEPS,)), DMA((CHIPS,)), DMA((CHIPS,))] * 4), DMA((2,)), DMA((2,)),
        ],
        compiler_params=pltpu.CompilerParams(
            collective_id=0, has_side_effects=True, vmem_limit_bytes=62 * 1024 * 1024,
        ),
    )(src_rows.T, src_accum.reshape(1, SRC), dst_rows, dst_accum.reshape(1, SHARD), relations.T, rel_ids, targets)
    (new_src, new_accum, new_rows, new_row_accum, loss) = hand_over(new_src, new_accum, new_rows, new_row_accum, loss)
    return (new_src.T, new_accum.reshape(SRC), new_rows, new_row_accum.reshape(SHARD), loss)


def solution(mesh):
    both = ("grp", "wide")
    placed = (P(both, None), P(both), P(both, None), P(both), P(), P(None, both), P(None, both))
    return jax.shard_map(
        shards, mesh=mesh, in_specs=placed,
        out_specs=(P(both, None), P(both), P(both, None), P(both), P(None, both)),
        check_vma=False,
    )
```
